512 devices in a mesh: ax: 16 (over y_hi, x), circ: 32 (over y_lo, z, core).
Axes of the slice: x: 4, y: 8 (y_hi: 4, y_lo: 2; y = y_hi * 2 + y_lo), z: 8, core: 2. Of those that a mesh axis runs over, the one named last changes fastest.
Arguments:
- displace: float32 [3, 512, 16384], P(None, 'ax', 'circ'), may hold values from -6 to 6
- load: float32 [3, 512, 16384], P(None, 'ax', 'circ'), may hold values from -6 to 6
- history: float32 [9, 512, 16384], P(None, 'ax', 'circ'), may hold values from -4 to 4
- stiffen: float32 [512, 16384], P('ax', 'circ'), may hold values from 0.2 to 4
- modulus: float32 [9, 9], replicated, may hold values from -2 to 2
- radial_slope: float32 [32, 32], replicated, may hold values from -1 to 1
- radial_basis: float32 [32, 32], replicated, may hold values from -1 to 1
- axial_eig: float32 [512], replicated, may hold values from 0.05 to 4
- cycle_eig: float32 [512], replicated, may hold values from 0.05 to 4
- radial_eig: float32 [32], replicated, may hold values from 0.05 to 4
Outputs:
- precond: float32 [3, 512, 16384], P(None, ('ax', 'circ'))
The draws below stay inside these ranges and needn't reach their ends.
All inputs are finite; a program needn't handle non-finite values.
Results may differ from the reference program's by a relative error of at most 0.000092.
Values sent between devices are 32-bit elements; how exact they have to be, the bound alone decides.
A program may use at most 64 MiB of HBM per device.

```python
import math
import jax
import jax.numpy as jnp
from jax import lax

NA = 512
NC = 512
R = 32


def block_levels(rng, shape, split, smallest, high):
    level, own = 1.0, jax.random.fold_in(rng, 6)
    for dim, parts in split:
        heights = jnp.exp(jax.random.uniform(jax.random.fold_in(own, dim), (parts,), jnp.float32, smallest / len(split), high / len(split)))
        level = level * jnp.repeat(heights, shape[dim] // parts).reshape([-1 if axis == dim else 1 for axis in range(len(shape))])
    return level


def normal_values(rng, extent, deviation, reach, shards=(), held_as=jnp.bfloat16):
    values = deviation * jax.random.normal(rng, extent, jnp.float32)
    if shards:
        values = values * block_levels(rng, extent, shards, -0.22, 0.18)
    return jnp.clip(values, -reach, reach).astype(held_as)


def setup_inputs(seed: int = 0) -> dict:
    streams_of = jax.random.split(jax.random.key(seed), 11)
    displace = normal_values(streams_of[0], (3, NA, NC * R), 1.0, 6.0, ((1, 16), (2, 32)), jnp.float32)
    load = normal_values(streams_of[1], (3, NA, NC * R), 1.0, 6.0, ((1, 16), (2, 32)), jnp.float32)
    history = normal_values(streams_of[2], (9, NA, NC * R), 0.5, 4.0, ((1, 16), (2, 32)), jnp.float32)
    stiffen = jnp.clip(jnp.exp(math.log(4.0) - 2.9957323 * jax.random.uniform(streams_of[3], (NA, NC * R), jnp.float32) ** block_levels(streams_of[3], (NA, NC * R), ((0, 16), (1, 32)), -0.2, 0.2)), 0.2, 4.0)
    modulus = normal_values(streams_of[4], (9, 9), 9 ** -0.5, 2.0, (), jnp.float32)
    radial_slope = normal_values(streams_of[5], (R, R), R ** -0.5, 1.0, (), jnp.float32)
    radial_basis = normal_values(streams_of[6], (R, R), R ** -0.5, 1.0, (), jnp.float32)
    axial_eig = jnp.clip(jnp.exp(jax.random.uniform(streams_of[7], (NA,), jnp.float32, math.log(0.05), math.log(4.0))), 0.05, 4.0)
    cycle_eig = jnp.clip(jnp.exp(jax.random.uniform(streams_of[8], (NC,), jnp.float32, math.log(0.05), math.log(4.0))), 0.05, 4.0)
    radial_eig = jnp.clip(jnp.exp(jax.random.uniform(streams_of[9], (R,), jnp.float32, math.log(0.05), math.log(4.0))), 0.05, 4.0)
    return dict(displace=displace, load=load, history=history, stiffen=stiffen, modulus=modulus, radial_slope=radial_slope, radial_basis=radial_basis, axial_eig=axial_eig, cycle_eig=cycle_eig, radial_eig=radial_eig)


def cycle_table(count):
    col = jnp.arange(count, dtype=jnp.int32)[:, None]
    mode = jnp.arange(count, dtype=jnp.int32)[None, :]
    half = count // 2
    folded = jnp.where(mode <= half, mode, mode - half)
    shift = jnp.where(mode <= half, 0.0, 0.5 * math.pi).astype(jnp.float32)
    scale_ends = jnp.where((mode == 0) | (mode == half), math.sqrt(1.0 / count), math.sqrt(2.0 / count)).astype(jnp.float32)
    phase = (col * folded % count).astype(jnp.float32) * (2.0 * math.pi / count)
    return jnp.cos(phase - shift) * scale_ends

def axial_table(rows, count):
    first = (rows + 1)[:, None]
    mode = jnp.arange(count, dtype=jnp.int32)[None, :] + 1
    phase = (first * mode % (2 * (count + 1))).astype(jnp.float32) * (math.pi / (count + 1))
    return jnp.sin(phase) * math.sqrt(2.0 / (count + 1))

def cycle_parts(field):
    left = jnp.roll(field, 1, axis=2)
    right = jnp.roll(field, -1, axis=2)
    return ((left + 4.0 * field + right) / 6.0, (right - left) * 0.5)

def row_smooth(field):
    padded = jnp.pad(field, ((0, 0), (1, 1), (0, 0), (0, 0)))
    return (padded[:, :-2] + 4.0 * padded[:, 1:-1] + padded[:, 2:]) / 6.0

def row_slope(field):
    padded = jnp.pad(field, ((0, 0), (1, 1), (0, 0), (0, 0)))
    return (padded[:, 2:] - padded[:, :-2]) * 0.5

def reference(displace, load, history, stiffen, modulus, radial_slope, radial_basis, axial_eig, cycle_eig, radial_eig):
    high = lax.Precision.HIGHEST
    shape4 = (NA, NC, R)
    field = displace.reshape((3,) + shape4)
    cycle_v, cycle_d = cycle_parts(field)
    smooth_v = row_smooth(cycle_v)
    radial_part = jnp.einsum('iacq,rq->iacr', smooth_v, radial_slope, precision=high)
    grads = jnp.concatenate([row_slope(cycle_v), row_smooth(cycle_d), radial_part], axis=0)
    mixed = jnp.einsum('mn,nacr->macr', modulus, grads, precision=high)
    stress = (1.0 + stiffen.reshape(shape4))[None] * mixed + history.reshape((9,) + shape4)
    first_v, unused_d = cycle_parts(stress[0:3])
    unused_v, second_d = cycle_parts(stress[3:6])
    third_v, unused_e = cycle_parts(stress[6:9])
    third = jnp.einsum('iacr,rq->iacq', row_smooth(third_v), radial_slope, precision=high)
    pull = -row_slope(first_v) - row_smooth(second_d) + third
    resid = load.reshape((3,) + shape4) - pull
    table_cycle = cycle_table(NC)
    table_axial = axial_table(jnp.arange(NA, dtype=jnp.int32), NA)
    spec = jnp.einsum('iacr,ck->iakr', resid, table_cycle, precision=high)
    spec = jnp.einsum('iakr,rm->iakm', spec, radial_basis, precision=high)
    spec = jnp.einsum('iakm,ab->ibkm', spec, table_axial, precision=high)
    denom = axial_eig[:, None, None] + cycle_eig[None, :, None] + radial_eig[None, None, :]
    scaled = spec / denom[None]
    back = jnp.einsum('ibkm,ab->iakm', scaled, table_axial, precision=high)
    back = jnp.einsum('iakm,rm->iakr', back, radial_basis, precision=high)
    back = jnp.einsum('iakr,ck->iacr', back, table_cycle, precision=high)
    return back.reshape(3, NA, NC * R)
```

```python
import math

import jax
import jax.numpy as jnp
import ml_dtypes
import numpy as np
from jax import lax
from jax.experimental import pallas as pl
from jax.experimental.pallas import tpu as pltpu
from jax.sharding import PartitionSpec as P

NA = 512
NC = 512
R = 32
NX = 16
NJ = 32
F32 = jnp.float32
BF16 = jnp.bfloat16
MESH = pl.DeviceIdType.MESH


def cycle_table():
    col = np.arange(NC)[:, None]
    mode = np.arange(NC)[None, :]
    half = NC // 2
    folded = np.where(mode <= half, mode, mode - half)
    shift = np.where(mode <= half, 0.0, 0.5 * np.pi)
    scale = np.where((mode == 0) | (mode == half), math.sqrt(1.0 / NC), math.sqrt(2.0 / NC))
    return np.cos((col * folded % NC) * (2.0 * np.pi / NC) - shift) * scale


def axial_table():
    first = (np.arange(NA) + 1)[:, None]
    mode = (np.arange(NA) + 1)[None, :]
    return np.sin((first * mode % (2 * (NA + 1))) * (np.pi / (NA + 1))) * math.sqrt(2.0 / (NA + 1))


def two_parts(table):
    table = table.astype(np.float32)
    high = table.astype(ml_dtypes.bfloat16)
    low = (table - high.astype(np.float32)).astype(ml_dtypes.bfloat16)
    return np.stack([high, low])


def tables():
    cyc, axi = cycle_table(), axial_table()
    q, cl, j = np.meshgrid(np.arange(4), np.arange(4), np.arange(NJ), indexing="ij")
    cycle_in = cyc[(16 * j + 4 * q + cl).reshape(-1)]
    a4, i, ah = np.meshgrid(np.arange(4), np.arange(NX), np.arange(8), indexing="ij")
    perm = (32 * i + 8 * a4 + ah).reshape(-1)
    c4, cg = np.meshgrid(np.arange(4), np.arange(128), indexing="ij")
    cycle_out = cyc.T[:, (4 * cg + c4).reshape(-1)]
    return np.stack([two_parts(cycle_in), two_parts(axi[perm]), two_parts(axi[:, perm]), two_parts(cycle_out)])


def roll(x, shift):
    return pltpu.roll(x, shift % x.shape[-1], x.ndim - 1)


def parts_of(x):
    high = x.astype(BF16)
    return high, (x - high.astype(F32)).astype(BF16)


def mm(a, b):
    return jnp.dot(a, b, preferred_element_type=F32)


def mm_t(a, b):
    return lax.dot_general(a, b, (((1,), (1,)), ((), ())), preferred_element_type=F32)


def dot3(x, high, low):
    xh, xl = parts_of(x)
    n = x.shape[0]
    both = mm(jnp.concatenate([xh, xl], axis=0), high)
    return both[:n] + (both[n:] + mm(xh, low))


def dot3_t(high, low, x):
    xh, xl = parts_of(x)
    n = high.shape[0]
    both = mm_t(jnp.concatenate([high, low], axis=0), xh)
    return both[:n] + (both[n:] + mm_t(high, xl))


def block_diag(x):
    wide = x + roll(x, 32)
    wide = wide + roll(wide, 64)
    full = jnp.concatenate([wide] * 4, axis=0)
    row = lax.broadcasted_iota(jnp.int32, (128, 128), 0) // 32
    lane = lax.broadcasted_iota(jnp.int32, (128, 128), 1) // 32
    return jnp.where(row == lane, full, 0.0)


def swap_groups(v):
    group = lax.broadcasted_iota(jnp.int32, v[0].shape, 1) // 32
    low_half = group < 2
    a0 = jnp.where(low_half, v[0], roll(v[2], 64))
    a2 = jnp.where(low_half, roll(v[0], 64), v[2])
    a1 = jnp.where(low_half, v[1], roll(v[3], 64))
    a3 = jnp.where(low_half, roll(v[1], 64), v[3])
    even = (group % 2) == 0
    u0 = jnp.where(even, a0, roll(a1, 32))
    u1 = jnp.where(even, roll(a0, -32), a1)
    u2 = jnp.where(even, a2, roll(a3, 32))
    u3 = jnp.where(even, roll(a2, -32), a3)
    return [u0, u1, u2, u3]


def tiles(x):
    return [x[:, 128 * t : 128 * (t + 1)] for t in range(x.shape[1] // 128)]


def rows(x, n):
    return [x[n * t : n * (t + 1)] for t in range(x.shape[0] // n)]


def smooth_a(up, mid, down):
    return (up + 4.0 * mid + down) * (1.0 / 6.0)


def slope_a(up, down):
    return (down - up) * 0.5


def smooth_c(x):
    return (roll(x, 32) + 4.0 * x + roll(x, -32)) * (1.0 / 6.0)


def slope_c(x):
    return (roll(x, -32) - roll(x, 32)) * 0.5


def gradients(windows, slope_t):
    first, second, plain = [], [], []
    for up, mid, down in windows:
        first.append(smooth_c(slope_a(up, down)))
        smooth = smooth_a(up, mid, down)
        second.append(slope_c(smooth))
        plain.append(smooth_c(smooth))
    stacked = jnp.concatenate([t for x in plain for t in tiles(x)], axis=0)
    mixed = rows(dot3(stacked, *slope_t), 40)
    third = [jnp.concatenate(mixed[6 * p : 6 * p + 6], axis=1) for p in range(3)]
    return first + second + third


def pulled(load, stress, p):
    up, _, down = stress(p)
    part = smooth_c(slope_a(up, down))
    part = part + slope_c(smooth_a(*stress(3 + p)))
    third = smooth_c(smooth_a(*stress(6 + p)))
    near = load + part[:, 128:640]
    return jnp.concatenate(tiles(near), axis=0), jnp.concatenate(tiles(third[:, 128:640]), axis=0)


def cycle_forward(parts, high, low):
    lhs = []
    for x in parts:
        lhs.append(jnp.concatenate(rows(x.T, 32), axis=1))
    y = dot3(jnp.concatenate(lhs, axis=0), high, low)
    out = []
    for p in range(3):
        block = tiles(y[32 * p : 32 * p + 32])
        out.append([swap_groups(rows(t, 8)) for t in block])
    return out


def axial_solve(parts, denom, forward, inverse):
    lhs = jnp.concatenate([jnp.concatenate(rows(x.T, 32), axis=1) for x in parts], axis=0)
    modes = dot3(lhs, *forward)
    modes = modes / jnp.concatenate([denom] * 3, axis=0)
    y = dot3(modes, *inverse)
    return [jnp.concatenate(tiles(x), axis=0).T for x in rows(y, 32)]


def cycle_inverse(parts, high, low):
    lhs = []
    for p in range(3):
        cols = [jnp.concatenate(swap_groups(parts[p][it]), axis=0) for it in range(4)]
        lhs.append(jnp.concatenate(cols, axis=1))
    return dot3(jnp.concatenate(lhs, axis=0), high, low)


def radial_inverse(parts, high, low):
    return dot3(jnp.concatenate([x.T for x in parts], axis=0), high, low)


def kernel(
    displace, load, history, stiffen, table, slope_ref, basis_ref, axial_ref, cycle_ref, modulus, radial,
    out,
    dext, hext, sext, load_v, table_v, pad_v, rsend, rtop, rbot, corner, stress_v,
    s1, r1, s2, r2, s3, r3, s4, r4, out_v,
    in_sem, table_sem, halo_send, halo_recv, a2a_send, a2a_recv, out_sem,
):
    i = lax.axis_index("ax")
    j = lax.axis_index("circ")
    up_i, down_i = lax.rem(i + NX - 1, NX), lax.rem(i + 1, NX)
    left_j, right_j = lax.rem(j + NJ - 1, NJ), lax.rem(j + 1, NJ)

    own = [
        pltpu.make_async_copy(displace, dext.at[:, 8:40, 128:640], in_sem.at[0]),
        pltpu.make_async_copy(history, hext.at[:, 8:40, 128:640], in_sem.at[1]),
        pltpu.make_async_copy(stiffen, sext.at[8:40, 128:640], in_sem.at[2]),
        pltpu.make_async_copy(load, load_v, in_sem.at[3]),
    ]
    for copy in own:
        copy.start()
    table_copies = [pltpu.make_async_copy(table.at[k], table_v.at[k], table_sem.at[k]) for k in range(4)]

    barrier = pltpu.get_barrier_semaphore()

    def greet_circ(s, carry):
        pl.semaphore_signal(barrier, inc=1, device_id=(i, lax.rem(j + s, NJ)), device_id_type=MESH)
        return carry

    def greet_ax(s, carry):
        pl.semaphore_signal(barrier, inc=1, device_id=(lax.rem(i + s, NX), j), device_id_type=MESH)
        return carry

    for di in (up_i, down_i):
        for dj in (left_j, right_j):
            pl.semaphore_signal(barrier, inc=1, device_id=(di, dj), device_id_type=MESH)
    lax.fori_loop(1, NX, greet_ax, 0)
    lax.fori_loop(1, NJ, greet_circ, 0)
    for copy in table_copies:
        copy.start()

    for copy in own[:3]:
        copy.wait()
    for side, (d0, h0) in enumerate(((8, 8), (38, 39))):
        for p in range(3):
            rsend[side, 2 * p : 2 * p + 2, :] = dext[p, d0 : d0 + 2, 128:640]
        for n in range(9):
            rsend[side, 6 + n : 7 + n, :] = hext[n, h0 : h0 + 1, 128:640]
        rsend[side, 15:16, :] = sext[h0 : h0 + 1, 128:640]

    pl.semaphore_wait(barrier, NJ - 1 + NX - 1 + 4)

    copies = []

    def send(src, dst, device):
        k = len(copies)
        copy = pltpu.make_async_remote_copy(
            src_ref=src, dst_ref=dst, send_sem=halo_send.at[k], recv_sem=halo_recv.at[k],
            device_id=device, device_id_type=MESH,
        )
        copy.start()
        copies.append(copy)

    send(rsend.at[1], rtop, (down_i, j))
    send(rsend.at[0], rbot, (up_i, j))
    send(displace.at[:, :, 384:512], dext.at[:, 8:40, 0:128], (i, right_j))
    send(displace.at[:, :, 0:128], dext.at[:, 8:40, 640:768], (i, left_j))
    send(history.at[:, :, 384:512], hext.at[:, 8:40, 0:128], (i, right_j))
    send(history.at[:, :, 0:128], hext.at[:, 8:40, 640:768], (i, left_j))
    send(stiffen.at[:, 384:512], sext.at[8:40, 0:128], (i, right_j))
    send(stiffen.at[:, 0:128], sext.at[8:40, 640:768], (i, left_j))
    send(rsend.at[1, :, 384:512], corner.at[0, 0], (down_i, right_j))
    send(rsend.at[1, :, 0:128], corner.at[0, 1], (down_i, left_j))
    send(rsend.at[0, :, 384:512], corner.at[1, 0], (up_i, right_j))
    send(rsend.at[0, :, 0:128], corner.at[1, 1], (up_i, left_j))

    pad_v[...] = jnp.zeros_like(pad_v)
    pad_v[0, :, 0:32] = slope_ref[...]
    pad_v[1, :, 0:32] = basis_ref[...]
    slope = block_diag(pad_v[0])
    slope_t = slope.T
    basis_t = block_diag(pad_v[1]).T
    slope, slope_t, basis_t = parts_of(slope), parts_of(slope_t), parts_of(basis_t)
    lane = lax.broadcasted_iota(jnp.int32, (32, NC), 1)
    row = lax.broadcasted_iota(jnp.int32, (32, NC), 0)
    picked = jnp.where(lane == row + 32 * i, jnp.broadcast_to(cycle_ref[...], (32, NC)), 0.0)
    denom = axial_ref[...] + jnp.sum(picked, axis=1, keepdims=True) + radial[j]

    for copy in copies:
        copy.wait_recv()
    not_first, not_last = i > 0, i < NX - 1
    for side, (ref, d0, h0, there) in enumerate(((rtop, 6, 7, not_first), (rbot, 40, 40, not_last))):
        whole = jnp.concatenate([corner[side, 0], ref[...], corner[side, 1]], axis=1)
        whole = jnp.where(there, whole, 0.0)
        for p in range(3):
            dext[p, d0 : d0 + 2, :] = whole[2 * p : 2 * p + 2]
        for n in range(9):
            hext[n, h0 : h0 + 1, :] = whole[6 + n : 7 + n]
        sext[h0 : h0 + 1, :] = whole[15:16]

    windows = [(dext[p, 6:46, :], dext[p, 7:47, :], dext[p, 8:48, :]) for p in range(3)]
    grads = gradients(windows, slope_t)
    inside = lax.broadcasted_iota(jnp.int32, (40, 128), 0)
    keep = ((inside > 0) | not_first) & ((inside < 33) | not_last)
    for t in range(6):
        cols = slice(128 * t, 128 * (t + 1))
        piece = [g[:, cols] for g in grads]
        factor = 1.0 + sext[7:47, cols]
        for m in range(9):
            total = modulus[m, 0] * piece[0]
            for n in range(1, 9):
                total = total + modulus[m, n] * piece[n]
            stress_v[m, :, cols] = jnp.where(keep, factor * total + hext[m, 7:47, cols], 0.0)

    def stress(m):
        return stress_v[m, 0:32, :], stress_v[m, 1:33, :], stress_v[m, 2:34, :]

    own[3].wait()
    near, far = [], []
    for p in range(3):
        a, b = pulled(load_v[p], stress, p)
        near.append(a)
        far.append(b)
    resid = jnp.concatenate(near, axis=0) - dot3(jnp.concatenate(far, axis=0), *slope)

    for p in range(3):
        mixed = dot3_t(*basis_t, resid[128 * p : 128 * (p + 1)])
        for cl in range(4):
            s1[:, 4 * p + cl, :] = mixed[32 * cl : 32 * cl + 32]

    def exchange(k, src, dst, count, me, device):
        pltpu.make_async_copy(src.at[me], dst.at[me], a2a_recv.at[k]).start()

        def push(s, carry):
            d = lax.rem(me + s, count)
            pltpu.make_async_remote_copy(
                src_ref=src.at[d], dst_ref=dst.at[me], send_sem=a2a_send.at[k], recv_sem=a2a_recv.at[k],
                device_id=device(d), device_id_type=MESH,
            ).start()
            return carry

        lax.fori_loop(1, count, push, 0)
        pltpu.make_async_copy(dst, dst, a2a_recv.at[k]).wait()

    on_circ = lambda d: (i, d)
    on_ax = lambda d: (d, j)

    exchange(0, s1, r1, NJ, j, on_circ)
    table_copies[0].wait()
    lines = [jnp.concatenate([r1[:, 4 * p + cl, :] for cl in range(4)], axis=0) for p in range(3)]
    blocks = cycle_forward(lines, table_v[0, 0], table_v[0, 1])
    for p in range(3):
        for it in range(4):
            for i4 in range(4):
                s2[4 * it + i4, p] = blocks[p][it][i4]

    exchange(1, s2, r2, NX, i, on_ax)
    table_copies[1].wait()
    table_copies[2].wait()
    lines = [r2[:, p].reshape(128, 128) for p in range(3)]
    solved = axial_solve(lines, denom, (table_v[1, 0], table_v[1, 1]), (table_v[2, 0], table_v[2, 1]))
    for p in range(3):
        s3[:, p] = solved[p].reshape(NX, 8, 128)

    exchange(2, s3, r3, NX, i, on_ax)
    table_copies[3].wait()
    blocks = [[[r3[4 * it + i4, p] for i4 in range(4)] for it in range(4)] for p in range(3)]
    y = cycle_inverse(blocks, table_v[3, 0], table_v[3, 1])
    for p in range(3):
        for c4 in range(4):
            s4[:, 4 * p + c4, :] = y[32 * p : 32 * p + 32, 128 * c4 : 128 * (c4 + 1)]

    exchange(3, s4, r4, NJ, j, on_circ)
    lines = [jnp.concatenate([r4[:, 4 * p + c4, :] for c4 in range(4)], axis=0) for p in range(3)]
    out_v[...] = radial_inverse(lines, *basis_t)
    last = pltpu.make_async_copy(out_v, out, out_sem.at[0])
    last.start()

    for copy in copies:
        copy.wait_send()
    for k, (ref, count) in enumerate(((s1, NJ), (s2, NX), (s3, NX), (s4, NJ))):
        sent = ref.at[pl.ds(0, count - 1)]
        pltpu.make_async_copy(sent, sent, a2a_send.at[k]).wait()
    last.wait()


def solution(mesh):
    table = tables()

    def body(displace, load, history, stiffen, modulus, slope, basis, axial, cycle, radial):
        hbm = pl.BlockSpec(memory_space=pl.ANY)
        vmem = pl.BlockSpec(memory_space=pltpu.VMEM)
        smem = pl.BlockSpec(memory_space=pltpu.SMEM)
        dma = pltpu.SemaphoreType.DMA
        out = pl.pallas_call(
            kernel,
            out_shape=jax.ShapeDtypeStruct((384, 128), F32),
            in_specs=[hbm] * 5 + [vmem] * 4 + [smem] * 2,
            out_specs=hbm,
            scratch_shapes=[
                pltpu.VMEM((3, 48, 768), F32),
                pltpu.VMEM((9, 48, 768), F32),
                pltpu.VMEM((48, 768), F32),
                pltpu.VMEM((3, 32, 512), F32),
                pltpu.VMEM((4, 2, 512, 512), BF16),
                pltpu.VMEM((2, 32, 128), F32),
                pltpu.VMEM((2, 16, 512), F32),
                pltpu.VMEM((16, 512), F32),
                pltpu.VMEM((16, 512), F32),
                pltpu.VMEM((2, 2, 16, 128), F32),
                pltpu.VMEM((9, 40, 768), F32),
                pltpu.VMEM((NJ, 12, 128), F32),
                pltpu.VMEM((NJ, 12, 128), F32),
                pltpu.VMEM((NX, 3, 8, 128), F32),
                pltpu.VMEM((NX, 3, 8, 128), F32),
                pltpu.VMEM((NX, 3, 8, 128), F32),
                pltpu.VMEM((NX, 3, 8, 128), F32),
                pltpu.VMEM((NJ, 12, 128), F32),
                pltpu.VMEM((NJ, 12, 128), F32),
                pltpu.VMEM((384, 128), F32),
                dma((4,)),
                dma((4,)),
                dma((12,)),
                dma((12,)),
                dma((4,)),
                dma((4,)),
                dma((1,)),
            ],
            compiler_params=pltpu.CompilerParams(
                collective_id=0, has_side_effects=True, vmem_limit_bytes=48 * 1024 * 1024
            ),
        )(
            displace, load, history, stiffen, jnp.asarray(table), slope, basis,
            axial.reshape(1, NA), cycle.reshape(1, NC), modulus, radial,
        )
        return out.reshape(3, 1, NC * R)

    return jax.shard_map(
        body,
        mesh=mesh,
        in_specs=(
            P(None, "ax", "circ"),
            P(None, "ax", "circ"),
            P(None, "ax", "circ"),
            P("ax", "circ"),
            P(),
            P(),
            P(),
            P(),
            P(),
            P(),
        ),
        out_specs=P(None, ("ax", "circ"), None),
        check_vma=False,
    )
```

```python
import math

import jax
import jax.numpy as jnp
import ml_dtypes
import numpy as np
from jax import lax
from jax.experimental import pallas as pl
from jax.experimental.pallas import tpu as pltpu
from jax.sharding import PartitionSpec as P

NA = 512
NC = 512
R = 32
NX = 16
NJ = 32
F32 = jnp.float32
BF16 = jnp.bfloat16
MESH = pl.DeviceIdType.MESH


def cycle_table():
    col = np.arange(NC)[:, None]
    mode = np.arange(NC)[None, :]
    half = NC // 2
    folded = np.where(mode <= half, mode, mode - half)
    shift = np.where(mode <= half, 0.0, 0.5 * np.pi)
    scale = np.where((mode == 0) | (mode == half), math.sqrt(1.0 / NC), math.sqrt(2.0 / NC))
    return np.cos((col * folded % NC) * (2.0 * np.pi / NC) - shift) * scale


def axial_table():
    first = (np.arange(NA) + 1)[:, None]
    mode = (np.arange(NA) + 1)[None, :]
    return np.sin((first * mode % (2 * (NA + 1))) * (np.pi / (NA + 1))) * math.sqrt(2.0 / (NA + 1))


def two_parts(table):
    table = table.astype(np.float32)
    high = table.astype(ml_dtypes.bfloat16)
    low = (table - high.astype(np.float32)).astype(ml_dtypes.bfloat16)
    return np.stack([high, low])


def tables():
    cyc, axi = cycle_table(), axial_table()
    q, cl, j = np.meshgrid(np.arange(4), np.arange(4), np.arange(NJ), indexing="ij")
    cycle_in = cyc[(16 * j + 4 * q + cl).reshape(-1)]
    a4, i, ah = np.meshgrid(np.arange(4), np.arange(NX), np.arange(8), indexing="ij")
    perm = (32 * i + 8 * a4 + ah).reshape(-1)
    c4, cg = np.meshgrid(np.arange(4), np.arange(128), indexing="ij")
    cycle_out = cyc.T[:, (4 * cg + c4).reshape(-1)]
    return np.stack([two_parts(cycle_in), two_parts(axi[perm]), two_parts(axi[:, perm]), two_parts(cycle_out)])


def roll(x, shift):
    return pltpu.roll(x, shift % x.shape[-1], x.ndim - 1)


def parts_of(x):
    high = x.astype(BF16)
    return high, (x - high.astype(F32)).astype(BF16)


def mm(a, b):
    return jnp.dot(a, b, preferred_element_type=F32)


def mm_t(a, b):
    return lax.dot_general(a, b, (((1,), (1,)), ((), ())), preferred_element_type=F32)


def dot3(x, high, low):
    xh, xl = parts_of(x)
    n = x.shape[0]
    both = mm(jnp.concatenate([xh, xl], axis=0), high)
    return both[:n] + (both[n:] + mm(xh, low))


def dot3_t(high, low, x):
    xh, xl = parts_of(x)
    n = high.shape[0]
    both = mm_t(jnp.concatenate([high, low], axis=0), xh)
    return both[:n] + (both[n:] + mm_t(high, xl))


def block_diag(x):
    wide = x + roll(x, 32)
    wide = wide + roll(wide, 64)
    full = jnp.concatenate([wide] * 4, axis=0)
    row = lax.broadcasted_iota(jnp.int32, (128, 128), 0) // 32
    lane = lax.broadcasted_iota(jnp.int32, (128, 128), 1) // 32
    return jnp.where(row == lane, full, 0.0)


def swap_groups(v):
    group = lax.broadcasted_iota(jnp.int32, v[0].shape, 1) // 32
    low_half = group < 2
    a0 = jnp.where(low_half, v[0], roll(v[2], 64))
    a2 = jnp.where(low_half, roll(v[0], 64), v[2])
    a1 = jnp.where(low_half, v[1], roll(v[3], 64))
    a3 = jnp.where(low_half, roll(v[1], 64), v[3])
    even = (group % 2) == 0
    u0 = jnp.where(even, a0, roll(a1, 32))
    u1 = jnp.where(even, roll(a0, -32), a1)
    u2 = jnp.where(even, a2, roll(a3, 32))
    u3 = jnp.where(even, roll(a2, -32), a3)
    return [u0, u1, u2, u3]


def tiles(x):
    return [x[:, 128 * t : 128 * (t + 1)] for t in range(x.shape[1] // 128)]


def rows(x, n):
    return [x[n * t : n * (t + 1)] for t in range(x.shape[0] // n)]


def smooth_a(up, mid, down):
    return (up + 4.0 * mid + down) * (1.0 / 6.0)


def slope_a(up, down):
    return (down - up) * 0.5


def smooth_c(x):
    return (roll(x, 32) + 4.0 * x + roll(x, -32)) * (1.0 / 6.0)


def slope_c(x):
    return (roll(x, -32) - roll(x, 32)) * 0.5


def gradients(windows, slope_t):
    first, second, plain = [], [], []
    for up, mid, down in windows:
        first.append(smooth_c(slope_a(up, down)))
        smooth = smooth_a(up, mid, down)
        second.append(slope_c(smooth))
        plain.append(smooth_c(smooth))
    stacked = jnp.concatenate([t for x in plain for t in tiles(x)], axis=0)
    mixed = rows(dot3(stacked, *slope_t), 40)
    third = [jnp.concatenate(mixed[6 * p : 6 * p + 6], axis=1) for p in range(3)]
    return first + second + third


def pulled(load, stress, p):
    up, _, down = stress(p)
    part = smooth_c(slope_a(up, down))
    part = part + slope_c(smooth_a(*stress(3 + p)))
    third = smooth_c(smooth_a(*stress(6 + p)))
    near = load + part[:, 128:640]
    return jnp.concatenate(tiles(near), axis=0), jnp.concatenate(tiles(third[:, 128:640]), axis=0)


def cycle_forward(parts, high, low):
    lhs = []
    for x in parts:
        lhs.append(jnp.concatenate(rows(x.T, 32), axis=1))
    y = dot3(jnp.concatenate(lhs, axis=0), high, low)
    out = []
    for p in range(3):
        block = tiles(y[32 * p : 32 * p + 32])
        out.append([swap_groups(rows(t, 8)) for t in block])
    return out


def axial_solve(parts, denom, forward, inverse):
    lhs = jnp.concatenate([jnp.concatenate(rows(x.T, 32), axis=1) for x in parts], axis=0)
    modes = dot3(lhs, *forward)
    modes = modes / jnp.concatenate([denom] * 3, axis=0)
    y = dot3(modes, *inverse)
    return [jnp.concatenate(tiles(x), axis=0).T for x in rows(y, 32)]


def cycle_inverse(parts, high, low):
    lhs = []
    for p in range(3):
        cols = [jnp.concatenate(swap_groups(parts[p][it]), axis=0) for it in range(4)]
        lhs.append(jnp.concatenate(cols, axis=1))
    return dot3(jnp.concatenate(lhs, axis=0), high, low)


def radial_inverse(parts, high, low):
    return dot3(jnp.concatenate([x.T for x in parts], axis=0), high, low)


def kernel(
    displace, load, history, stiffen, table, slope_hbm, basis_hbm, axial_hbm, cycle_hbm, modulus_hbm, radial_hbm,
    out_v,
    slope_ref, basis_ref, axial_ref, cycle_ref, modulus, radial,
    dext, hext, sext, load_v, table_v, pad_v, rsend, rtop, rbot, corner, stress_v,
    s1, r1, s2, r2, s3, r3, s4, r4,
    in_sem, table_sem, halo_send, halo_recv, a2a_send, a2a_recv,
):
    i = lax.axis_index("ax")
    j = lax.axis_index("circ")
    up_i, down_i = lax.rem(i + NX - 1, NX), lax.rem(i + 1, NX)
    left_j, right_j = lax.rem(j + NJ - 1, NJ), lax.rem(j + 1, NJ)

    own = [
        pltpu.make_async_copy(displace, dext.at[:, 8:40, 128:640], in_sem.at[0]),
        pltpu.make_async_copy(history, hext.at[:, 8:40, 128:640], in_sem.at[1]),
        pltpu.make_async_copy(stiffen, sext.at[8:40, 128:640], in_sem.at[2]),
        pltpu.make_async_copy(slope_hbm, slope_ref, in_sem.at[3]),
        pltpu.make_async_copy(basis_hbm, basis_ref, in_sem.at[4]),
        pltpu.make_async_copy(axial_hbm, axial_ref, in_sem.at[5]),
        pltpu.make_async_copy(cycle_hbm, cycle_ref, in_sem.at[6]),
        pltpu.make_async_copy(modulus_hbm, modulus, in_sem.at[7]),
        pltpu.make_async_copy(radial_hbm, radial, in_sem.at[8]),
        pltpu.make_async_copy(load, load_v, in_sem.at[9]),
    ]
    for copy in own:
        copy.start()
    table_copies = [pltpu.make_async_copy(table.at[k], table_v.at[k], table_sem.at[k]) for k in range(4)]

    barrier = pltpu.get_barrier_semaphore()

    def greet_circ(s, carry):
        pl.semaphore_signal(barrier, inc=1, device_id=(i, lax.rem(j + s, NJ)), device_id_type=MESH)
        return carry

    def greet_ax(s, carry):
        pl.semaphore_signal(barrier, inc=1, device_id=(lax.rem(i + s, NX), j), device_id_type=MESH)
        return carry

    for di in (up_i, down_i):
        for dj in (left_j, right_j):
            pl.semaphore_signal(barrier, inc=1, device_id=(di, dj), device_id_type=MESH)
    lax.fori_loop(1, NX, greet_ax, 0)
    lax.fori_loop(1, NJ, greet_circ, 0)
    for copy in table_copies:
        copy.start()

    for copy in own[:3]:
        copy.wait()
    for side, (d0, h0) in enumerate(((8, 8), (38, 39))):
        for p in range(3):
            rsend[side, 2 * p : 2 * p + 2, :] = dext[p, d0 : d0 + 2, 128:640]
        for n in range(9):
            rsend[side, 6 + n : 7 + n, :] = hext[n, h0 : h0 + 1, 128:640]
        rsend[side, 15:16, :] = sext[h0 : h0 + 1, 128:640]

    pl.semaphore_wait(barrier, NJ - 1 + NX - 1 + 4)

    copies = []

    def send(src, dst, device):
        k = len(copies)
        copy = pltpu.make_async_remote_copy(
            src_ref=src, dst_ref=dst, send_sem=halo_send.at[k], recv_sem=halo_recv.at[k],
            device_id=device, device_id_type=MESH,
        )
        copy.start()
        copies.append(copy)

    send(rsend.at[1], rtop, (down_i, j))
    send(rsend.at[0], rbot, (up_i, j))
    send(displace.at[:, :, 384:512], dext.at[:, 8:40, 0:128], (i, right_j))
    send(displace.at[:, :, 0:128], dext.at[:, 8:40, 640:768], (i, left_j))
    send(history.at[:, :, 384:512], hext.at[:, 8:40, 0:128], (i, right_j))
    send(history.at[:, :, 0:128], hext.at[:, 8:40, 640:768], (i, left_j))
    send(stiffen.at[:, 384:512], sext.at[8:40, 0:128], (i, right_j))
    send(stiffen.at[:, 0:128], sext.at[8:40, 640:768], (i, left_j))
    send(rsend.at[1, :, 384:512], corner.at[0, 0], (down_i, right_j))
    send(rsend.at[1, :, 0:128], corner.at[0, 1], (down_i, left_j))
    send(rsend.at[0, :, 384:512], corner.at[1, 0], (up_i, right_j))
    send(rsend.at[0, :, 0:128], corner.at[1, 1], (up_i, left_j))

    for copy in own[3:]:
        copy.wait()
    pad_v[...] = jnp.zeros_like(pad_v)
    pad_v[0, :, 0:32] = slope_ref[...]
    pad_v[1, :, 0:32] = basis_ref[...]
    slope = block_diag(pad_v[0])
    slope_t = slope.T
    basis_t = block_diag(pad_v[1]).T
    slope, slope_t, basis_t = parts_of(slope), parts_of(slope_t), parts_of(basis_t)
    lane = lax.broadcasted_iota(jnp.int32, (32, NC), 1)
    row = lax.broadcasted_iota(jnp.int32, (32, NC), 0)
    picked = jnp.where(lane == row + 32 * i, jnp.broadcast_to(cycle_ref[...], (32, NC)), 0.0)
    denom = axial_ref[...] + jnp.sum(picked, axis=1, keepdims=True) + radial[j]

    for copy in copies:
        copy.wait_recv()
    not_first, not_last = i > 0, i < NX - 1
    for side, (ref, d0, h0, there) in enumerate(((rtop, 6, 7, not_first), (rbot, 40, 40, not_last))):
        whole = jnp.concatenate([corner[side, 0], ref[...], corner[side, 1]], axis=1)
        whole = jnp.where(there, whole, 0.0)
        for p in range(3):
            dext[p, d0 : d0 + 2, :] = whole[2 * p : 2 * p + 2]
        for n in range(9):
            hext[n, h0 : h0 + 1, :] = whole[6 + n : 7 + n]
        sext[h0 : h0 + 1, :] = whole[15:16]

    windows = [(dext[p, 6:46, :], dext[p, 7:47, :], dext[p, 8:48, :]) for p in range(3)]
    grads = gradients(windows, slope_t)
    inside = lax.broadcasted_iota(jnp.int32, (40, 128), 0)
    keep = ((inside > 0) | not_first) & ((inside < 33) | not_last)
    for t in range(6):
        cols = slice(128 * t, 128 * (t + 1))
        piece = [g[:, cols] for g in grads]
        factor = 1.0 + sext[7:47, cols]
        for m in range(9):
            total = modulus[m, 0] * piece[0]
            for n in range(1, 9):
                total = total + modulus[m, n] * piece[n]
            stress_v[m, :, cols] = jnp.where(keep, factor * total + hext[m, 7:47, cols], 0.0)

    def stress(m):
        return stress_v[m, 0:32, :], stress_v[m, 1:33, :], stress_v[m, 2:34, :]

    near, far = [], []
    for p in range(3):
        a, b = pulled(load_v[p], stress, p)
        near.append(a)
        far.append(b)
    resid = jnp.concatenate(near, axis=0) - dot3(jnp.concatenate(far, axis=0), *slope)

    for p in range(3):
        mixed = dot3_t(*basis_t, resid[128 * p : 128 * (p + 1)])
        for cl in range(4):
            s1[:, 4 * p + cl, :] = mixed[32 * cl : 32 * cl + 32]

    def exchange(k, src, dst, count, me, device):
        pltpu.make_async_copy(src.at[me], dst.at[me], a2a_recv.at[k]).start()

        def push(s, carry):
            d = lax.rem(me + s, count)
            pltpu.make_async_remote_copy(
                src_ref=src.at[d], dst_ref=dst.at[me], send_sem=a2a_send.at[k], recv_sem=a2a_recv.at[k],
                device_id=device(d), device_id_type=MESH,
            ).start()
            return carry

        lax.fori_loop(1, count, push, 0)
        pltpu.make_async_copy(dst, dst, a2a_recv.at[k]).wait()

    on_circ = lambda d: (i, d)
    on_ax = lambda d: (d, j)

    exchange(0, s1, r1, NJ, j, on_circ)
    table_copies[0].wait()
    lines = [jnp.concatenate([r1[:, 4 * p + cl, :] for cl in range(4)], axis=0) for p in range(3)]
    blocks = cycle_forward(lines, table_v[0, 0], table_v[0, 1])
    for p in range(3):
        for it in range(4):
            for i4 in range(4):
                s2[4 * it + i4, p] = blocks[p][it][i4]

    exchange(1, s2, r2, NX, i, on_ax)
    table_copies[1].wait()
    table_copies[2].wait()
    lines = [r2[:, p].reshape(128, 128) for p in range(3)]
    solved = axial_solve(lines, denom, (table_v[1, 0], table_v[1, 1]), (table_v[2, 0], table_v[2, 1]))
    for p in range(3):
        s3[:, p] = solved[p].reshape(NX, 8, 128)

    exchange(2, s3, r3, NX, i, on_ax)
    table_copies[3].wait()
    blocks = [[[r3[4 * it + i4, p] for i4 in range(4)] for it in range(4)] for p in range(3)]
    y = cycle_inverse(blocks, table_v[3, 0], table_v[3, 1])
    for p in range(3):
        for c4 in range(4):
            s4[:, 4 * p + c4, :] = y[32 * p : 32 * p + 32, 128 * c4 : 128 * (c4 + 1)]

    exchange(3, s4, r4, NJ, j, on_circ)
    lines = [jnp.concatenate([r4[:, 4 * p + c4, :] for c4 in range(4)], axis=0) for p in range(3)]
    out_v[...] = radial_inverse(lines, *basis_t)

    for copy in copies:
        copy.wait_send()
    for k, (ref, count) in enumerate(((s1, NJ), (s2, NX), (s3, NX), (s4, NJ))):
        sent = ref.at[pl.ds(0, count - 1)]
        pltpu.make_async_copy(sent, sent, a2a_send.at[k]).wait()


def solution(mesh):
    table = tables()

    def body(displace, load, history, stiffen, modulus, slope, basis, axial, cycle, radial):
        hbm = pl.BlockSpec(memory_space=pltpu.HBM)
        dma = pltpu.SemaphoreType.DMA
        out = pl.pallas_call(
            kernel,
            out_shape=jax.ShapeDtypeStruct((384, 128), F32),
            in_specs=[hbm] * 11,
            out_specs=pl.BlockSpec(memory_space=pltpu.VMEM),
            scratch_shapes=[
                pltpu.VMEM((R, R), F32),
                pltpu.VMEM((R, R), F32),
                pltpu.VMEM((1, NA), F32),
                pltpu.VMEM((1, NC), F32),
                pltpu.SMEM((9, 9), F32),
                pltpu.SMEM((R,), F32),
                pltpu.VMEM((3, 48, 768), F32),
                pltpu.VMEM((9, 48, 768), F32),
                pltpu.VMEM((48, 768), F32),
                pltpu.VMEM((3, 32, 512), F32),
                pltpu.VMEM((4, 2, 512, 512), BF16),
                pltpu.VMEM((2, 32, 128), F32),
                pltpu.VMEM((2, 16, 512), F32),
                pltpu.VMEM((16, 512), F32),
                pltpu.VMEM((16, 512), F32),
                pltpu.VMEM((2, 2, 16, 128), F32),
                pltpu.VMEM((9, 40, 768), F32),
                pltpu.VMEM((NJ, 12, 128), F32),
                pltpu.VMEM((NJ, 12, 128), F32),
                pltpu.VMEM((NX, 3, 8, 128), F32),
                pltpu.VMEM((NX, 3, 8, 128), F32),
                pltpu.VMEM((NX, 3, 8, 128), F32),
                pltpu.VMEM((NX, 3, 8, 128), F32),
                pltpu.VMEM((NJ, 12, 128), F32),
                pltpu.VMEM((NJ, 12, 128), F32),
                dma((10,)),
                dma((4,)),
                dma((12,)),
                dma((12,)),
                dma((4,)),
                dma((4,)),
            ],
            compiler_params=pltpu.CompilerParams(
                collective_id=0, has_side_effects=True, vmem_limit_bytes=60 * 1024 * 1024
            ),
        )(
            displace, load, history, stiffen, jnp.asarray(table), slope, basis,
            axial.reshape(1, NA), cycle.reshape(1, NC), modulus, radial,
        )
        return out.reshape(3, 1, NC * R)

    return jax.shard_map(
        body,
        mesh=mesh,
        in_specs=(
            P(None, "ax", "circ"),
            P(None, "ax", "circ"),
            P(None, "ax", "circ"),
            P("ax", "circ"),
            P(),
            P(),
            P(),
            P(),
            P(),
            P(),
        ),
        out_specs=P(None, ("ax", "circ"), None),
        check_vma=False,
    )
```

```python
import math

import jax
import jax.numpy as jnp
import ml_dtypes
import numpy as np
from jax import lax
from jax.experimental import pallas as pl
from jax.experimental.pallas import tpu as pltpu
from jax.sharding import PartitionSpec as P

NA = 512
NC = 512
R = 32
NX = 16
NJ = 32
F32 = jnp.float32
BF16 = jnp.bfloat16
MESH = pl.DeviceIdType.MESH


def cycle_table():
    col = np.arange(NC)[:, None]
    mode = np.arange(NC)[None, :]
    half = NC // 2
    folded = np.where(mode <= half, mode, mode - half)
    shift = np.where(mode <= half, 0.0, 0.5 * np.pi)
    scale = np.where((mode == 0) | (mode == half), math.sqrt(1.0 / NC), math.sqrt(2.0 / NC))
    return np.cos((col * folded % NC) * (2.0 * np.pi / NC) - shift) * scale


def axial_table():
    first = (np.arange(NA) + 1)[:, None]
    mode = (np.arange(NA) + 1)[None, :]
    return np.sin((first * mode % (2 * (NA + 1))) * (np.pi / (NA + 1))) * math.sqrt(2.0 / (NA + 1))


def two_parts(table):
    table = table.astype(np.float32)
    high = table.astype(ml_dtypes.bfloat16)
    low = (table - high.astype(np.float32)).astype(ml_dtypes.bfloat16)
    return np.stack([high, low])


def tables():
    cyc, axi = cycle_table(), axial_table()
    q, cl, j = np.meshgrid(np.arange(4), np.arange(4), np.arange(NJ), indexing="ij")
    cycle_in = cyc[(16 * j + 4 * q + cl).reshape(-1)]
    a4, i, ah = np.meshgrid(np.arange(4), np.arange(NX), np.arange(8), indexing="ij")
    perm = (32 * i + 8 * a4 + ah).reshape(-1)
    c4, cg = np.meshgrid(np.arange(4), np.arange(128), indexing="ij")
    cycle_out = cyc.T[:, (4 * cg + c4).reshape(-1)]
    return np.stack([two_parts(cycle_in), two_parts(axi[perm]), two_parts(axi[:, perm]), two_parts(cycle_out)])


def roll(x, shift):
    return pltpu.roll(x, shift % x.shape[-1], x.ndim - 1)


def parts_of(x):
    high = x.astype(BF16)
    return high, (x - high.astype(F32)).astype(BF16)


def mm(a, b):
    return jnp.dot(a, b, preferred_element_type=F32)


def mm_t(a, b):
    return lax.dot_general(a, b, (((1,), (1,)), ((), ())), preferred_element_type=F32)


def dot3(x, high, low):
    xh, xl = parts_of(x)
    n = x.shape[0]
    both = mm(jnp.concatenate([xh, xl], axis=0), high)
    return both[:n] + (both[n:] + mm(xh, low))


def dot3_t(high, low, x):
    xh, xl = parts_of(x)
    n = high.shape[0]
    both = mm_t(jnp.concatenate([high, low], axis=0), xh)
    return both[:n] + (both[n:] + mm_t(high, xl))


def block_diag(x):
    wide = x + roll(x, 32)
    wide = wide + roll(wide, 64)
    full = jnp.concatenate([wide] * 4, axis=0)
    row = lax.broadcasted_iota(jnp.int32, (128, 128), 0) // 32
    lane = lax.broadcasted_iota(jnp.int32, (128, 128), 1) // 32
    return jnp.where(row == lane, full, 0.0)


def swap_groups(v):
    group = lax.broadcasted_iota(jnp.int32, v[0].shape, 1) // 32
    low_half = group < 2
    a0 = jnp.where(low_half, v[0], roll(v[2], 64))
    a2 = jnp.where(low_half, roll(v[0], 64), v[2])
    a1 = jnp.where(low_half, v[1], roll(v[3], 64))
    a3 = jnp.where(low_half, roll(v[1], 64), v[3])
    even = (group % 2) == 0
    u0 = jnp.where(even, a0, roll(a1, 32))
    u1 = jnp.where(even, roll(a0, -32), a1)
    u2 = jnp.where(even, a2, roll(a3, 32))
    u3 = jnp.where(even, roll(a2, -32), a3)
    return [u0, u1, u2, u3]


def tiles(x):
    return [x[:, 128 * t : 128 * (t + 1)] for t in range(x.shape[1] // 128)]


def rows(x, n):
    return [x[n * t : n * (t + 1)] for t in range(x.shape[0] // n)]


def smooth_a(up, mid, down):
    return (up + 4.0 * mid + down) * (1.0 / 6.0)


def slope_a(up, down):
    return (down - up) * 0.5


def smooth_c(x):
    return (roll(x, 32) + 4.0 * x + roll(x, -32)) * (1.0 / 6.0)


def slope_c(x):
    return (roll(x, -32) - roll(x, 32)) * 0.5


def gradients(windows, slope_t):
    first, second, plain = [], [], []
    for up, mid, down in windows:
        first.append(smooth_c(slope_a(up, down)))
        smooth = smooth_a(up, mid, down)
        second.append(slope_c(smooth))
        plain.append(smooth_c(smooth))
    stacked = jnp.concatenate([t for x in plain for t in tiles(x)], axis=0)
    mixed = rows(dot3(stacked, *slope_t), 40)
    third = [jnp.concatenate(mixed[6 * p : 6 * p + 6], axis=1) for p in range(3)]
    return first + second + third


def pulled(load, stress, p):
    up, _, down = stress(p)
    part = smooth_c(slope_a(up, down))
    part = part + slope_c(smooth_a(*stress(3 + p)))
    third = smooth_c(smooth_a(*stress(6 + p)))
    near = load + part[:, 128:640]
    return jnp.concatenate(tiles(near), axis=0), jnp.concatenate(tiles(third[:, 128:640]), axis=0)


def cycle_forward(x, high, low):
    y = dot3(jnp.concatenate(rows(x.T, 32), axis=1), high, low)
    return [swap_groups(rows(t, 8)) for t in tiles(y)]


def axial_solve(x, denom, forward, inverse):
    modes = dot3(jnp.concatenate(rows(x.T, 32), axis=1), *forward)
    y = dot3(modes / denom, *inverse)
    return jnp.concatenate(tiles(y), axis=0).T


def cycle_inverse(blocks, high, low):
    cols = [jnp.concatenate(swap_groups(four), axis=0) for four in blocks]
    return dot3(jnp.concatenate(cols, axis=1), high, low)


def pack_columns(fields, last):
    lane = lax.broadcasted_iota(jnp.int32, (32, 128), 1)

    def move(x, width, at):
        start = 128 - width if last else 0
        return roll(x, at - start) if at != start else x

    two = jnp.where(lane < 64, move(fields[0], 64, 0), move(fields[1], 64, 64))
    mixed = jnp.where(lane < 96, move(fields[3], 32, 64), move(fields[4], 32, 96))
    out = [two, jnp.where(lane < 64, move(fields[2], 64, 0), mixed)]
    for first in (5, 9):
        low = jnp.where(lane < 32, move(fields[first], 32, 0), move(fields[first + 1], 32, 32))
        high = jnp.where(lane < 96, move(fields[first + 2], 32, 64), move(fields[first + 3], 32, 96))
        out.append(jnp.where(lane < 64, low, high))
    return out


def unpack_columns(packed, last):
    def move(x, width, at):
        end = 128 - width if last else 0
        return roll(x, end - at) if at != end else x

    out = [move(packed[0], 64, 0), move(packed[0], 64, 64), move(packed[1], 64, 0)]
    out += [move(packed[1], 32, 64), move(packed[1], 32, 96)]
    for t in (2, 3):
        out += [move(packed[t], 32, 32 * g) for g in range(4)]
    return out


def kernel(
    displace, load, history, stiffen, table, slope_hbm, basis_hbm, axial_hbm, cycle_hbm, modulus_hbm, radial_hbm,
    out_v,
    slope_ref, basis_ref, axial_ref, cycle_ref, modulus, radial,
    dext, hext, sext, load_v, table_v, pad_v, rsend, csend, rtop, rbot, cleft, cright, corner, stress_v,
    s1, r1, s2, r2, s3, r3, s4, r4,
    in_sem, table_sem, halo_send, halo_recv, a2a_send, a2a_recv,
):
    i = lax.axis_index("ax")
    j = lax.axis_index("circ")
    up_i, down_i = lax.rem(i + NX - 1, NX), lax.rem(i + 1, NX)
    left_j, right_j = lax.rem(j + NJ - 1, NJ), lax.rem(j + 1, NJ)

    own = [
        pltpu.make_async_copy(displace, dext.at[:, 8:40, 128:640], in_sem.at[0]),
        pltpu.make_async_copy(history, hext.at[:, 8:40, 128:640], in_sem.at[1]),
        pltpu.make_async_copy(stiffen, sext.at[8:40, 128:640], in_sem.at[2]),
        pltpu.make_async_copy(slope_hbm, slope_ref, in_sem.at[3]),
        pltpu.make_async_copy(basis_hbm, basis_ref, in_sem.at[4]),
        pltpu.make_async_copy(axial_hbm, axial_ref, in_sem.at[5]),
        pltpu.make_async_copy(cycle_hbm, cycle_ref, in_sem.at[6]),
        pltpu.make_async_copy(modulus_hbm, modulus, in_sem.at[7]),
        pltpu.make_async_copy(radial_hbm, radial, in_sem.at[8]),
        pltpu.make_async_copy(load, load_v, in_sem.at[9]),
    ]
    for copy in own:
        copy.start()
    table_copies = [pltpu.make_async_copy(table.at[k], table_v.at[k], table_sem.at[k]) for k in range(4)]

    barrier = pltpu.get_barrier_semaphore()

    def greet_circ(s, carry):
        pl.semaphore_signal(barrier, inc=1, device_id=(i, lax.rem(j + s, NJ)), device_id_type=MESH)
        return carry

    def greet_ax(s, carry):
        pl.semaphore_signal(barrier, inc=1, device_id=(lax.rem(i + s, NX), j), device_id_type=MESH)
        return carry

    for di in (up_i, down_i):
        for dj in (left_j, right_j):
            pl.semaphore_signal(barrier, inc=1, device_id=(di, dj), device_id_type=MESH)
    lax.fori_loop(1, NX, greet_ax, 0)
    lax.fori_loop(1, NJ, greet_circ, 0)
    for copy in table_copies:
        copy.start()

    for copy in own[:3]:
        copy.wait()
    for side, (d0, h0) in enumerate(((8, 8), (38, 39))):
        for p in range(3):
            rsend[side, 2 * p : 2 * p + 2, :] = dext[p, d0 : d0 + 2, 128:640]
        for n in range(9):
            rsend[side, 6 + n : 7 + n, :] = hext[n, h0 : h0 + 1, 128:640]
        rsend[side, 15:16, :] = sext[h0 : h0 + 1, 128:640]

    for side, cols in enumerate((slice(128, 256), slice(512, 640))):
        edge = [dext[p, 8:40, cols] for p in range(3)] + [hext[n, 8:40, cols] for n in range(9)] + [sext[8:40, cols]]
        for t, value in enumerate(pack_columns(edge, side == 1)):
            csend[side, t] = value

    pl.semaphore_wait(barrier, NJ - 1 + NX - 1 + 4)

    copies = []

    def send(src, dst, device):
        k = len(copies)
        copy = pltpu.make_async_remote_copy(
            src_ref=src, dst_ref=dst, send_sem=halo_send.at[k], recv_sem=halo_recv.at[k],
            device_id=device, device_id_type=MESH,
        )
        copy.start()
        copies.append(copy)

    send(rsend.at[1], rtop, (down_i, j))
    send(rsend.at[0], rbot, (up_i, j))
    send(csend.at[1], cleft, (i, right_j))
    send(csend.at[0], cright, (i, left_j))
    send(rsend.at[1, :, 384:512], corner.at[0, 0], (down_i, right_j))
    send(rsend.at[1, :, 0:128], corner.at[0, 1], (down_i, left_j))
    send(rsend.at[0, :, 384:512], corner.at[1, 0], (up_i, right_j))
    send(rsend.at[0, :, 0:128], corner.at[1, 1], (up_i, left_j))

    for copy in own[3:]:
        copy.wait()
    pad_v[...] = jnp.zeros_like(pad_v)
    pad_v[0, :, 0:32] = slope_ref[...]
    pad_v[1, :, 0:32] = basis_ref[...]
    slope = block_diag(pad_v[0])
    slope_t = slope.T
    basis_t = block_diag(pad_v[1]).T
    slope, slope_t, basis_t = parts_of(slope), parts_of(slope_t), parts_of(basis_t)
    lane = lax.broadcasted_iota(jnp.int32, (32, NC), 1)
    row = lax.broadcasted_iota(jnp.int32, (32, NC), 0)
    picked = jnp.where(lane == row + 32 * i, jnp.broadcast_to(cycle_ref[...], (32, NC)), 0.0)
    denom = axial_ref[...] + jnp.sum(picked, axis=1, keepdims=True) + radial[j]

    for copy in copies:
        copy.wait_recv()
    not_first, not_last = i > 0, i < NX - 1
    for ref, cols, left in ((cleft, slice(0, 128), True), (cright, slice(640, 768), False)):
        fields = unpack_columns([ref[t] for t in range(4)], left)
        for p in range(3):
            dext[p, 8:40, cols] = fields[p]
        for n in range(9):
            hext[n, 8:40, cols] = fields[3 + n]
        sext[8:40, cols] = fields[12]
    for side, (ref, d0, h0, there) in enumerate(((rtop, 6, 7, not_first), (rbot, 40, 40, not_last))):
        whole = jnp.concatenate([corner[side, 0], ref[...], corner[side, 1]], axis=1)
        whole = jnp.where(there, whole, 0.0)
        for p in range(3):
            dext[p, d0 : d0 + 2, :] = whole[2 * p : 2 * p + 2]
        for n in range(9):
            hext[n, h0 : h0 + 1, :] = whole[6 + n : 7 + n]
        sext[h0 : h0 + 1, :] = whole[15:16]

    windows = [(dext[p, 6:46, :], dext[p, 7:47, :], dext[p, 8:48, :]) for p in range(3)]
    grads = gradients(windows, slope_t)
    inside = lax.broadcasted_iota(jnp.int32, (40, 128), 0)
    keep = ((inside > 0) | not_first) & ((inside < 33) | not_last)
    for t in range(6):
        cols = slice(128 * t, 128 * (t + 1))
        piece = [g[:, cols] for g in grads]
        factor = 1.0 + sext[7:47, cols]
        for m in range(9):
            total = modulus[m, 0] * piece[0]
            for n in range(1, 9):
                total = total + modulus[m, n] * piece[n]
            stress_v[m, :, cols] = jnp.where(keep, factor * total + hext[m, 7:47, cols], 0.0)

    def stress(m):
        return stress_v[m, 0:32, :], stress_v[m, 1:33, :], stress_v[m, 2:34, :]

    def start(k, p, src, dst, count, me, device):
        pltpu.make_async_copy(src.at[p, me], dst.at[p, me], a2a_recv.at[k, p]).start()

        def push(s, carry):
            d = lax.rem(me + s, count)
            pltpu.make_async_remote_copy(
                src_ref=src.at[p, d], dst_ref=dst.at[p, me], send_sem=a2a_send.at[k], recv_sem=a2a_recv.at[k, p],
                device_id=device(d), device_id_type=MESH,
            ).start()
            return carry

        lax.fori_loop(1, count, push, 0)

    def arrived(k, p, dst):
        pltpu.make_async_copy(dst.at[p], dst.at[p], a2a_recv.at[k, p]).wait()

    on_circ = lambda d: (i, d)
    on_ax = lambda d: (d, j)

    for p in range(3):
        near, far = pulled(load_v[p], stress, p)
        mixed = dot3_t(*basis_t, near - dot3(far, *slope))
        for cl in range(4):
            s1[p, :, cl, :] = mixed[32 * cl : 32 * cl + 32]
        start(0, p, s1, r1, NJ, j, on_circ)

    table_copies[0].wait()
    for p in range(3):
        arrived(0, p, r1)
        line = jnp.concatenate([r1[p, :, cl, :] for cl in range(4)], axis=0)
        for it, four in enumerate(cycle_forward(line, table_v[0, 0], table_v[0, 1])):
            for i4 in range(4):
                s2[p, 4 * it + i4] = four[i4]
        start(1, p, s2, r2, NX, i, on_ax)

    table_copies[1].wait()
    table_copies[2].wait()
    for p in range(3):
        arrived(1, p, r2)
        line = r2[p].reshape(128, 128)
        solved = axial_solve(line, denom, (table_v[1, 0], table_v[1, 1]), (table_v[2, 0], table_v[2, 1]))
        s3[p] = solved.reshape(NX, 8, 128)
        start(2, p, s3, r3, NX, i, on_ax)

    table_copies[3].wait()
    for p in range(3):
        arrived(2, p, r3)
        blocks = [[r3[p, 4 * it + i4] for i4 in range(4)] for it in range(4)]
        y = cycle_inverse(blocks, table_v[3, 0], table_v[3, 1])
        for c4 in range(4):
            s4[p, :, c4, :] = y[:, 128 * c4 : 128 * (c4 + 1)]
        start(3, p, s4, r4, NJ, j, on_circ)

    for p in range(3):
        arrived(3, p, r4)
        line = jnp.concatenate([r4[p, :, c4, :] for c4 in range(4)], axis=0)
        out_v[128 * p : 128 * (p + 1), :] = dot3(line.T, *basis_t)

    for copy in copies:
        copy.wait_send()
    for k, (ref, count) in enumerate(((s1, NJ), (s2, NX), (s3, NX), (s4, NJ))):
        sent = ref.at[:, pl.ds(0, count - 1)]
        pltpu.make_async_copy(sent, sent, a2a_send.at[k]).wait()


def solution(mesh):
    table = tables()

    def body(displace, load, history, stiffen, modulus, slope, basis, axial, cycle, radial):
        hbm = pl.BlockSpec(memory_space=pltpu.HBM)
        dma = pltpu.SemaphoreType.DMA
        out = pl.pallas_call(
            kernel,
            out_shape=jax.ShapeDtypeStruct((384, 128), F32),
            in_specs=[hbm] * 11,
            out_specs=pl.BlockSpec(memory_space=pltpu.VMEM),
            scratch_shapes=[
                pltpu.VMEM((R, R), F32),
                pltpu.VMEM((R, R), F32),
                pltpu.VMEM((1, NA), F32),
                pltpu.VMEM((1, NC), F32),
                pltpu.SMEM((9, 9), F32),
                pltpu.SMEM((R,), F32),
                pltpu.VMEM((3, 48, 768), F32),
                pltpu.VMEM((9, 48, 768), F32),
                pltpu.VMEM((48, 768), F32),
                pltpu.VMEM((3, 32, 512), F32),
                pltpu.VMEM((4, 2, 512, 512), BF16),
                pltpu.VMEM((2, 32, 128), F32),
                pltpu.VMEM((2, 16, 512), F32),
                pltpu.VMEM((2, 4, 32, 128), F32),
                pltpu.VMEM((16, 512), F32),
                pltpu.VMEM((16, 512), F32),
                pltpu.VMEM((4, 32, 128), F32),
                pltpu.VMEM((4, 32, 128), F32),
                pltpu.VMEM((2, 2, 16, 128), F32),
                pltpu.VMEM((9, 40, 768), F32),
                pltpu.VMEM((3, NJ, 4, 128), F32),
                pltpu.VMEM((3, NJ, 4, 128), F32),
                pltpu.VMEM((3, NX, 8, 128), F32),
                pltpu.VMEM((3, NX, 8, 128), F32),
                pltpu.VMEM((3, NX, 8, 128), F32),
                pltpu.VMEM((3, NX, 8, 128), F32),
                pltpu.VMEM((3, NJ, 4, 128), F32),
                pltpu.VMEM((3, NJ, 4, 128), F32),
                dma((10,)),
                dma((4,)),
                dma((8,)),
                dma((8,)),
                dma((4,)),
                dma((4, 3)),
            ],
            compiler_params=pltpu.CompilerParams(
                collective_id=0, has_side_effects=True, vmem_limit_bytes=60 * 1024 * 1024
            ),
        )(
            displace, load, history, stiffen, jnp.asarray(table), slope, basis,
            axial.reshape(1, NA), cycle.reshape(1, NC), modulus, radial,
        )
        return out.reshape(3, 1, NC * R)

    return jax.shard_map(
        body,
        mesh=mesh,
        in_specs=(
            P(None, "ax", "circ"),
            P(None, "ax", "circ"),
            P(None, "ax", "circ"),
            P("ax", "circ"),
            P(),
            P(),
            P(),
            P(),
            P(),
            P(),
        ),
        out_specs=P(None, ("ax", "circ"), None),
        check_vma=False,
    )
```

```python
import math

import jax
import jax.numpy as jnp
import ml_dtypes
import numpy as np
from jax import lax
from jax.experimental import pallas as pl
from jax.experimental.pallas import tpu as pltpu
from jax.sharding import PartitionSpec as P

NA = 512
NC = 512
R = 32
NX = 16
NJ = 32
F32 = jnp.float32
BF16 = jnp.bfloat16
MESH = pl.DeviceIdType.MESH


def cycle_table():
    col = np.arange(NC)[:, None]
    mode = np.arange(NC)[None, :]
    half = NC // 2
    folded = np.where(mode <= half, mode, mode - half)
    shift = np.where(mode <= half, 0.0, 0.5 * np.pi)
    scale = np.where((mode == 0) | (mode == half), math.sqrt(1.0 / NC), math.sqrt(2.0 / NC))
    return np.cos((col * folded % NC) * (2.0 * np.pi / NC) - shift) * scale


def axial_table():
    first = (np.arange(NA) + 1)[:, None]
    mode = (np.arange(NA) + 1)[None, :]
    return np.sin((first * mode % (2 * (NA + 1))) * (np.pi / (NA + 1))) * math.sqrt(2.0 / (NA + 1))


def two_parts(table):
    table = table.astype(np.float32)
    high = table.astype(ml_dtypes.bfloat16)
    low = (table - high.astype(np.float32)).astype(ml_dtypes.bfloat16)
    return np.stack([high, low])


def tables():
    cyc, axi = cycle_table(), axial_table()
    q, cl, j = np.meshgrid(np.arange(4), np.arange(4), np.arange(NJ), indexing="ij")
    cycle_in = cyc[(16 * j + 4 * q + cl).reshape(-1)]
    a4, i, ah = np.meshgrid(np.arange(4), np.arange(NX), np.arange(8), indexing="ij")
    perm = (32 * i + 8 * a4 + ah).reshape(-1)
    c4, cg = np.meshgrid(np.arange(4), np.arange(128), indexing="ij")
    cycle_out = cyc.T[:, (4 * cg + c4).reshape(-1)]
    return np.stack([two_parts(cycle_in), two_parts(axi[perm]), two_parts(axi[:, perm]), two_parts(cycle_out)])


def roll(x, shift):
    return pltpu.roll(x, shift % x.shape[-1], x.ndim - 1)


def parts_of(x):
    high = x.astype(BF16)
    return high, (x - high.astype(F32)).astype(BF16)


def mm(a, b):
    return jnp.dot(a, b, preferred_element_type=F32)


def mm_t(a, b):
    return lax.dot_general(a, b, (((1,), (1,)), ((), ())), preferred_element_type=F32)


def dot3(x, high, low):
    xh, xl = parts_of(x)
    n = x.shape[0]
    both = mm(jnp.concatenate([xh, xl], axis=0), high)
    return both[:n] + (both[n:] + mm(xh, low))


def dot3_t(high, low, x):
    xh, xl = parts_of(x)
    n = high.shape[0]
    both = mm_t(jnp.concatenate([high, low], axis=0), xh)
    return both[:n] + (both[n:] + mm_t(high, xl))


def block_diag(x):
    wide = x + roll(x, 32)
    wide = wide + roll(wide, 64)
    full = jnp.concatenate([wide] * 4, axis=0)
    row = lax.broadcasted_iota(jnp.int32, (128, 128), 0) // 32
    lane = lax.broadcasted_iota(jnp.int32, (128, 128), 1) // 32
    return jnp.where(row == lane, full, 0.0)


def swap_groups(v):
    group = lax.broadcasted_iota(jnp.int32, v[0].shape, 1) // 32
    low_half = group < 2
    a0 = jnp.where(low_half, v[0], roll(v[2], 64))
    a2 = jnp.where(low_half, roll(v[0], 64), v[2])
    a1 = jnp.where(low_half, v[1], roll(v[3], 64))
    a3 = jnp.where(low_half, roll(v[1], 64), v[3])
    even = (group % 2) == 0
    u0 = jnp.where(even, a0, roll(a1, 32))
    u1 = jnp.where(even, roll(a0, -32), a1)
    u2 = jnp.where(even, a2, roll(a3, 32))
    u3 = jnp.where(even, roll(a2, -32), a3)
    return [u0, u1, u2, u3]


def tiles(x):
    return [x[:, 128 * t : 128 * (t + 1)] for t in range(x.shape[1] // 128)]


def rows(x, n):
    return [x[n * t : n * (t + 1)] for t in range(x.shape[0] // n)]


def smooth_a(up, mid, down):
    return (up + 4.0 * mid + down) * (1.0 / 6.0)


def slope_a(up, down):
    return (down - up) * 0.5


def smooth_c(x):
    return (roll(x, 32) + 4.0 * x + roll(x, -32)) * (1.0 / 6.0)


def slope_c(x):
    return (roll(x, -32) - roll(x, 32)) * 0.5


def gradients(windows, slope_t):
    first, second, plain = [], [], []
    for up, mid, down in windows:
        first.append(smooth_c(slope_a(up, down)))
        smooth = smooth_a(up, mid, down)
        second.append(slope_c(smooth))
        plain.append(smooth_c(smooth))
    stacked = jnp.concatenate([t for x in plain for t in tiles(x)], axis=0)
    mixed = rows(dot3(stacked, *slope_t), 40)
    third = [jnp.concatenate(mixed[6 * p : 6 * p + 6], axis=1) for p in range(3)]
    return first + second + third


def pulled(load, stress, p):
    up, _, down = stress(p)
    part = smooth_c(slope_a(up, down))
    part = part + slope_c(smooth_a(*stress(3 + p)))
    third = smooth_c(smooth_a(*stress(6 + p)))
    near = load + part[:, 128:640]
    return jnp.concatenate(tiles(near), axis=0), jnp.concatenate(tiles(third[:, 128:640]), axis=0)


def cycle_forward(x, high, low):
    y = dot3(jnp.concatenate(rows(x.T, 32), axis=1), high, low)
    return [swap_groups(rows(t, 8)) for t in tiles(y)]


def axial_solve(x, denom, forward, inverse):
    modes = dot3(jnp.concatenate(rows(x.T, 32), axis=1), *forward)
    y = dot3(modes / denom, *inverse)
    return jnp.concatenate(tiles(y), axis=0).T


def cycle_inverse(blocks, high, low):
    cols = [jnp.concatenate(swap_groups(four), axis=0) for four in blocks]
    return dot3(jnp.concatenate(cols, axis=1), high, low)


def pack_columns(fields, last):
    lane = lax.broadcasted_iota(jnp.int32, (32, 128), 1)

    def move(x, width, at):
        start = 128 - width if last else 0
        return roll(x, at - start) if at != start else x

    two = jnp.where(lane < 64, move(fields[0], 64, 0), move(fields[1], 64, 64))
    mixed = jnp.where(lane < 96, move(fields[3], 32, 64), move(fields[4], 32, 96))
    out = [two, jnp.where(lane < 64, move(fields[2], 64, 0), mixed)]
    for first in (5, 9):
        low = jnp.where(lane < 32, move(fields[first], 32, 0), move(fields[first + 1], 32, 32))
        high = jnp.where(lane < 96, move(fields[first + 2], 32, 64), move(fields[first + 3], 32, 96))
        out.append(jnp.where(lane < 64, low, high))
    return out


def unpack_columns(packed, last):
    def move(x, width, at):
        end = 128 - width if last else 0
        return roll(x, end - at) if at != end else x

    out = [move(packed[0], 64, 0), move(packed[0], 64, 64), move(packed[1], 64, 0)]
    out += [move(packed[1], 32, 64), move(packed[1], 32, 96)]
    for t in (2, 3):
        out += [move(packed[t], 32, 32 * g) for g in range(4)]
    return out


def kernel(
    displace, load, history, stiffen, table, slope_hbm, basis_hbm, axial_hbm, cycle_hbm, modulus_hbm, radial_hbm,
    out_v,
    slope_ref, basis_ref, axial_ref, cycle_ref, modulus, radial,
    dext, hext, sext, load_v, table_v, pad_v, rsend, csend, rtop, rbot, cleft, cright, corner, stress_v,
    s1, r1, s2, r2, s3, r3, s4, r4,
    in_sem, table_sem, halo_send, halo_recv, a2a_send, a2a_recv, known,
):
    i = lax.axis_index("ax")
    j = lax.axis_index("circ")
    up_i, down_i = lax.rem(i + NX - 1, NX), lax.rem(i + 1, NX)
    left_j, right_j = lax.rem(j + NJ - 1, NJ), lax.rem(j + 1, NJ)

    own = [
        pltpu.make_async_copy(displace, dext.at[:, 8:40, 128:640], in_sem.at[0]),
        pltpu.make_async_copy(history, hext.at[:, 8:40, 128:640], in_sem.at[1]),
        pltpu.make_async_copy(stiffen, sext.at[8:40, 128:640], in_sem.at[2]),
        pltpu.make_async_copy(slope_hbm, slope_ref, in_sem.at[3]),
        pltpu.make_async_copy(basis_hbm, basis_ref, in_sem.at[4]),
        pltpu.make_async_copy(axial_hbm, axial_ref, in_sem.at[5]),
        pltpu.make_async_copy(cycle_hbm, cycle_ref, in_sem.at[6]),
        pltpu.make_async_copy(modulus_hbm, modulus, in_sem.at[7]),
        pltpu.make_async_copy(radial_hbm, radial, in_sem.at[8]),
        pltpu.make_async_copy(load, load_v, in_sem.at[9]),
    ]
    for copy in own:
        copy.start()
    table_copies = [pltpu.make_async_copy(table.at[k], table_v.at[k], table_sem.at[k]) for k in range(4)]

    barrier = pltpu.get_barrier_semaphore()

    def near_z(side, step):
        y_lo, z, core = lax.div(j, 16), lax.rem(lax.div(j, 2), 8), lax.rem(j, 2)
        y_lo = lax.rem(y_lo + side // 2, 2)
        core = lax.rem(core + side % 2, 2)
        return y_lo * 16 + lax.rem(z + step, 8) * 2 + core

    def signal(sem, di, dj):
        pl.semaphore_signal(sem, inc=1, device_id=(di, dj), device_id_type=MESH)

    for di in (up_i, down_i):
        for dj in (left_j, right_j, j):
            signal(barrier, di, dj)
    for side in range(4):
        for step in (7, 1, 0):
            if side or step:
                signal(barrier, i, near_z(side, step))
    for copy in table_copies:
        copy.start()

    for copy in own[:3]:
        copy.wait()
    for side, (d0, h0) in enumerate(((8, 8), (38, 39))):
        for p in range(3):
            rsend[side, 2 * p : 2 * p + 2, :] = dext[p, d0 : d0 + 2, 128:640]
        for n in range(9):
            rsend[side, 6 + n : 7 + n, :] = hext[n, h0 : h0 + 1, 128:640]
        rsend[side, 15:16, :] = sext[h0 : h0 + 1, 128:640]

    for side, cols in enumerate((slice(128, 256), slice(512, 640))):
        edge = [dext[p, 8:40, cols] for p in range(3)] + [hext[n, 8:40, cols] for n in range(9)] + [sext[8:40, cols]]
        for t, value in enumerate(pack_columns(edge, side == 1)):
            csend[side, t] = value

    pl.semaphore_wait(barrier, 17)

    copies = []

    def send(src, dst, device):
        k = len(copies)
        copy = pltpu.make_async_remote_copy(
            src_ref=src, dst_ref=dst, send_sem=halo_send.at[k], recv_sem=halo_recv.at[k],
            device_id=device, device_id_type=MESH,
        )
        copy.start()
        copies.append(copy)

    send(rsend.at[1], rtop, (down_i, j))
    send(rsend.at[0], rbot, (up_i, j))
    send(csend.at[1], cleft, (i, right_j))
    send(csend.at[0], cright, (i, left_j))
    send(rsend.at[1, :, 384:512], corner.at[0, 0], (down_i, right_j))
    send(rsend.at[1, :, 0:128], corner.at[0, 1], (down_i, left_j))
    send(rsend.at[0, :, 384:512], corner.at[1, 0], (up_i, right_j))
    send(rsend.at[0, :, 0:128], corner.at[1, 1], (up_i, left_j))

    def tell_z(k, step):
        for way in (step, 8 - step):
            signal(known.at[k], i, near_z(0, way))

    def tell_ax(k, step):
        for way in (step, NX - step):
            signal(known.at[k], lax.rem(i + way, NX), j)

    def hear(k):
        pl.semaphore_wait(known.at[k], 2)

    tell_z(0, 1)
    tell_ax(2, 1)
    for copy in own[3:]:
        copy.wait()
    pad_v[...] = jnp.zeros_like(pad_v)
    pad_v[0, :, 0:32] = slope_ref[...]
    pad_v[1, :, 0:32] = basis_ref[...]
    slope = block_diag(pad_v[0])
    slope_t = slope.T
    basis_t = block_diag(pad_v[1]).T
    slope, slope_t, basis_t = parts_of(slope), parts_of(slope_t), parts_of(basis_t)
    lane = lax.broadcasted_iota(jnp.int32, (32, NC), 1)
    row = lax.broadcasted_iota(jnp.int32, (32, NC), 0)
    picked = jnp.where(lane == row + 32 * i, jnp.broadcast_to(cycle_ref[...], (32, NC)), 0.0)
    denom = axial_ref[...] + jnp.sum(picked, axis=1, keepdims=True) + radial[j]

    hear(0)
    tell_z(1, 2)
    hear(2)
    tell_ax(3, 2)
    for copy in copies:
        copy.wait_recv()
    not_first, not_last = i > 0, i < NX - 1
    for ref, cols, left in ((cleft, slice(0, 128), True), (cright, slice(640, 768), False)):
        fields = unpack_columns([ref[t] for t in range(4)], left)
        for p in range(3):
            dext[p, 8:40, cols] = fields[p]
        for n in range(9):
            hext[n, 8:40, cols] = fields[3 + n]
        sext[8:40, cols] = fields[12]
    for side, (ref, d0, h0, there) in enumerate(((rtop, 6, 7, not_first), (rbot, 40, 40, not_last))):
        whole = jnp.concatenate([corner[side, 0], ref[...], corner[side, 1]], axis=1)
        whole = jnp.where(there, whole, 0.0)
        for p in range(3):
            dext[p, d0 : d0 + 2, :] = whole[2 * p : 2 * p + 2]
        for n in range(9):
            hext[n, h0 : h0 + 1, :] = whole[6 + n : 7 + n]
        sext[h0 : h0 + 1, :] = whole[15:16]

    windows = [(dext[p, 6:46, :], dext[p, 7:47, :], dext[p, 8:48, :]) for p in range(3)]
    grads = gradients(windows, slope_t)
    inside = lax.broadcasted_iota(jnp.int32, (40, 128), 0)
    keep = ((inside > 0) | not_first) & ((inside < 33) | not_last)
    for t in range(6):
        cols = slice(128 * t, 128 * (t + 1))
        piece = [g[:, cols] for g in grads]
        factor = 1.0 + sext[7:47, cols]
        for m in range(9):
            total = modulus[m, 0] * piece[0]
            for n in range(1, 9):
                total = total + modulus[m, n] * piece[n]
            stress_v[m, :, cols] = jnp.where(keep, factor * total + hext[m, 7:47, cols], 0.0)

    def stress(m):
        return stress_v[m, 0:32, :], stress_v[m, 1:33, :], stress_v[m, 2:34, :]

    def start(k, p, src, dst, count, me, device):
        pltpu.make_async_copy(src.at[p, me], dst.at[p, me], a2a_recv.at[k, p]).start()

        def push(s, carry):
            d = lax.rem(me + s, count)
            pltpu.make_async_remote_copy(
                src_ref=src.at[p, d], dst_ref=dst.at[p, me], send_sem=a2a_send.at[k], recv_sem=a2a_recv.at[k, p],
                device_id=device(d), device_id_type=MESH,
            ).start()
            return carry

        lax.fori_loop(1, count, push, 0)

    def arrived(k, p, dst):
        pltpu.make_async_copy(dst.at[p], dst.at[p], a2a_recv.at[k, p]).wait()

    on_circ = lambda d: (i, d)
    on_ax = lambda d: (d, j)

    for p in range(3):
        near, far = pulled(load_v[p], stress, p)
        mixed = dot3_t(*basis_t, near - dot3(far, *slope))
        for cl in range(4):
            s1[p, :, cl, :] = mixed[32 * cl : 32 * cl + 32]
        if p == 0:
            hear(1)
        start(0, p, s1, r1, NJ, j, on_circ)

    hear(3)
    tell_ax(4, 4)
    table_copies[0].wait()
    for p in range(3):
        arrived(0, p, r1)
        line = jnp.concatenate([r1[p, :, cl, :] for cl in range(4)], axis=0)
        for it, four in enumerate(cycle_forward(line, table_v[0, 0], table_v[0, 1])):
            for i4 in range(4):
                s2[p, 4 * it + i4] = four[i4]
        if p == 0:
            hear(4)
        start(1, p, s2, r2, NX, i, on_ax)

    table_copies[1].wait()
    table_copies[2].wait()
    for p in range(3):
        arrived(1, p, r2)
        line = r2[p].reshape(128, 128)
        solved = axial_solve(line, denom, (table_v[1, 0], table_v[1, 1]), (table_v[2, 0], table_v[2, 1]))
        s3[p] = solved.reshape(NX, 8, 128)
        start(2, p, s3, r3, NX, i, on_ax)

    table_copies[3].wait()
    for p in range(3):
        arrived(2, p, r3)
        blocks = [[r3[p, 4 * it + i4] for i4 in range(4)] for it in range(4)]
        y = cycle_inverse(blocks, table_v[3, 0], table_v[3, 1])
        for c4 in range(4):
            s4[p, :, c4, :] = y[:, 128 * c4 : 128 * (c4 + 1)]
        start(3, p, s4, r4, NJ, j, on_circ)

    for p in range(3):
        arrived(3, p, r4)
        line = jnp.concatenate([r4[p, :, c4, :] for c4 in range(4)], axis=0)
        out_v[128 * p : 128 * (p + 1), :] = dot3(line.T, *basis_t)

    for copy in copies:
        copy.wait_send()
    for k, (ref, count) in enumerate(((s1, NJ), (s2, NX), (s3, NX), (s4, NJ))):
        sent = ref.at[:, pl.ds(0, count - 1)]
        pltpu.make_async_copy(sent, sent, a2a_send.at[k]).wait()


def solution(mesh):
    table = tables()

    def body(displace, load, history, stiffen, modulus, slope, basis, axial, cycle, radial):
        hbm = pl.BlockSpec(memory_space=pltpu.HBM)
        dma = pltpu.SemaphoreType.DMA
        out = pl.pallas_call(
            kernel,
            out_shape=pltpu.VMEM((384, 128), F32),
            in_specs=[hbm] * 11,
            out_specs=pl.BlockSpec(memory_space=pltpu.VMEM),
            scratch_shapes=[
                pltpu.VMEM((R, R), F32),
                pltpu.VMEM((R, R), F32),
                pltpu.VMEM((1, NA), F32),
                pltpu.VMEM((1, NC), F32),
                pltpu.SMEM((9, 9), F32),
                pltpu.SMEM((R,), F32),
                pltpu.VMEM((3, 48, 768), F32),
                pltpu.VMEM((9, 48, 768), F32),
                pltpu.VMEM((48, 768), F32),
                pltpu.VMEM((3, 32, 512), F32),
                pltpu.VMEM((4, 2, 512, 512), BF16),
                pltpu.VMEM((2, 32, 128), F32),
                pltpu.VMEM((2, 16, 512), F32),
                pltpu.VMEM((2, 4, 32, 128), F32),
                pltpu.VMEM((16, 512), F32),
                pltpu.VMEM((16, 512), F32),
                pltpu.VMEM((4, 32, 128), F32),
                pltpu.VMEM((4, 32, 128), F32),
                pltpu.VMEM((2, 2, 16, 128), F32),
                pltpu.VMEM((9, 40, 768), F32),
                pltpu.VMEM((3, NJ, 4, 128), F32),
                pltpu.VMEM((3, NJ, 4, 128), F32),
                pltpu.VMEM((3, NX, 8, 128), F32),
                pltpu.VMEM((3, NX, 8, 128), F32),
                pltpu.VMEM((3, NX, 8, 128), F32),
                pltpu.VMEM((3, NX, 8, 128), F32),
                pltpu.VMEM((3, NJ, 4, 128), F32),
                pltpu.VMEM((3, NJ, 4, 128), F32),
                dma((10,)),
                dma((4,)),
                dma((8,)),
                dma((8,)),
                dma((4,)),
                dma((4, 3)),
                pltpu.SemaphoreType.REGULAR((5,)),
            ],
            compiler_params=pltpu.CompilerParams(
                collective_id=0, has_side_effects=True, vmem_limit_bytes=60 * 1024 * 1024
            ),
        )(
            displace, load, history, stiffen, jnp.asarray(table), slope, basis,
            axial.reshape(1, NA), cycle.reshape(1, NC), modulus, radial,
        )
        return out.reshape(3, 1, NC * R)

    return jax.shard_map(
        body,
        mesh=mesh,
        in_specs=(
            P(None, "ax", "circ"),
            P(None, "ax", "circ"),
            P(None, "ax", "circ"),
            P("ax", "circ"),
            P(),
            P(),
            P(),
            P(),
            P(),
            P(),
        ),
        out_specs=P(None, ("ax", "circ"), None),
        check_vma=False,
    )
```

```python
import math

import jax
import jax.numpy as jnp
import ml_dtypes
import numpy as np
from jax import lax
from jax.experimental import pallas as pl
from jax.experimental.pallas import tpu as pltpu
from jax.sharding import PartitionSpec as P

NA = 512
NC = 512
R = 32
NX = 16
NJ = 32
F32 = jnp.float32
BF16 = jnp.bfloat16
MESH = pl.DeviceIdType.MESH


def cycle_table():
    col = np.arange(NC)[:, None]
    mode = np.arange(NC)[None, :]
    half = NC // 2
    folded = np.where(mode <= half, mode, mode - half)
    shift = np.where(mode <= half, 0.0, 0.5 * np.pi)
    scale = np.where((mode == 0) | (mode == half), math.sqrt(1.0 / NC), math.sqrt(2.0 / NC))
    return np.cos((col * folded % NC) * (2.0 * np.pi / NC) - shift) * scale


def axial_table():
    first = (np.arange(NA) + 1)[:, None]
    mode = (np.arange(NA) + 1)[None, :]
    return np.sin((first * mode % (2 * (NA + 1))) * (np.pi / (NA + 1))) * math.sqrt(2.0 / (NA + 1))


def two_parts(table):
    table = table.astype(np.float32)
    high = table.astype(ml_dtypes.bfloat16)
    low = (table - high.astype(np.float32)).astype(ml_dtypes.bfloat16)
    return np.stack([high, low])


def tables():
    cyc, axi = cycle_table(), axial_table()
    q, cl, j = np.meshgrid(np.arange(4), np.arange(4), np.arange(NJ), indexing="ij")
    cycle_in = cyc[(16 * j + 4 * q + cl).reshape(-1)]
    a4, i, ah = np.meshgrid(np.arange(4), np.arange(NX), np.arange(8), indexing="ij")
    perm = (32 * i + 8 * a4 + ah).reshape(-1)
    c4, cg = np.meshgrid(np.arange(4), np.arange(128), indexing="ij")
    cycle_out = cyc.T[:, (4 * cg + c4).reshape(-1)]
    return np.stack([two_parts(cycle_in), two_parts(axi[perm]), two_parts(axi[:, perm]), two_parts(cycle_out)])


def roll(x, shift):
    return pltpu.roll(x, shift % x.shape[-1], x.ndim - 1)


def parts_of(x):
    high = x.astype(BF16)
    return high, (x - high.astype(F32)).astype(BF16)


def mm(a, b):
    return jnp.dot(a, b, preferred_element_type=F32)


def mm_t(a, b):
    return lax.dot_general(a, b, (((1,), (1,)), ((), ())), preferred_element_type=F32)


def dot3(x, high, low):
    xh, xl = parts_of(x)
    n = x.shape[0]
    both = mm(jnp.concatenate([xh, xl], axis=0), high)
    return both[:n] + (both[n:] + mm(xh, low))


def dot3_t(high, low, x):
    xh, xl = parts_of(x)
    n = high.shape[0]
    both = mm_t(jnp.concatenate([high, low], axis=0), xh)
    return both[:n] + (both[n:] + mm_t(high, xl))


def block_diag(x):
    wide = x + roll(x, 32)
    wide = wide + roll(wide, 64)
    full = jnp.concatenate([wide] * 4, axis=0)
    row = lax.broadcasted_iota(jnp.int32, (128, 128), 0) // 32
    lane = lax.broadcasted_iota(jnp.int32, (128, 128), 1) // 32
    return jnp.where(row == lane, full, 0.0)


def swap_groups(v):
    group = lax.broadcasted_iota(jnp.int32, v[0].shape, 1) // 32
    low_half = group < 2
    a0 = jnp.where(low_half, v[0], roll(v[2], 64))
    a2 = jnp.where(low_half, roll(v[0], 64), v[2])
    a1 = jnp.where(low_half, v[1], roll(v[3], 64))
    a3 = jnp.where(low_half, roll(v[1], 64), v[3])
    even = (group % 2) == 0
    u0 = jnp.where(even, a0, roll(a1, 32))
    u1 = jnp.where(even, roll(a0, -32), a1)
    u2 = jnp.where(even, a2, roll(a3, 32))
    u3 = jnp.where(even, roll(a2, -32), a3)
    return [u0, u1, u2, u3]


def tiles(x):
    return [x[:, 128 * t : 128 * (t + 1)] for t in range(x.shape[1] // 128)]


def rows(x, n):
    return [x[n * t : n * (t + 1)] for t in range(x.shape[0] // n)]


def smooth_a(up, mid, down):
    return (up + 4.0 * mid + down) * (1.0 / 6.0)


def slope_a(up, down):
    return (down - up) * 0.5


def smooth_c(x):
    return (roll(x, 32) + 4.0 * x + roll(x, -32)) * (1.0 / 6.0)


def slope_c(x):
    return (roll(x, -32) - roll(x, 32)) * 0.5


def gradients(windows, slope_t):
    first, second, plain = [], [], []
    for up, mid, down in windows:
        first.append(smooth_c(slope_a(up, down)))
        smooth = smooth_a(up, mid, down)
        second.append(slope_c(smooth))
        plain.append(smooth_c(smooth))
    stacked = jnp.concatenate([t for x in plain for t in tiles(x)], axis=0)
    mixed = rows(dot3(stacked, *slope_t), 40)
    third = [jnp.concatenate(mixed[6 * p : 6 * p + 6], axis=1) for p in range(3)]
    return first + second + third


def pulled(load, stress, p):
    up, _, down = stress(p)
    part = smooth_c(slope_a(up, down))
    part = part + slope_c(smooth_a(*stress(3 + p)))
    third = smooth_c(smooth_a(*stress(6 + p)))
    near = load + part[:, 128:640]
    return jnp.concatenate(tiles(near), axis=0), jnp.concatenate(tiles(third[:, 128:640]), axis=0)


def cycle_forward(x, high, low):
    y = dot3(jnp.concatenate(rows(x.T, 32), axis=1), high, low)
    return [swap_groups(rows(t, 8)) for t in tiles(y)]


def axial_solve(x, denom, forward, inverse):
    modes = dot3(jnp.concatenate(rows(x.T, 32), axis=1), *forward)
    y = dot3(modes / denom, *inverse)
    return jnp.concatenate(tiles(y), axis=0).T


def cycle_inverse(blocks, high, low):
    cols = [jnp.concatenate(swap_groups(four), axis=0) for four in blocks]
    return dot3(jnp.concatenate(cols, axis=1), high, low)


def pack_columns(fields, last):
    lane = lax.broadcasted_iota(jnp.int32, (32, 128), 1)

    def move(x, width, at):
        start = 128 - width if last else 0
        return roll(x, at - start) if at != start else x

    two = jnp.where(lane < 64, move(fields[0], 64, 0), move(fields[1], 64, 64))
    mixed = jnp.where(lane < 96, move(fields[3], 32, 64), move(fields[4], 32, 96))
    out = [two, jnp.where(lane < 64, move(fields[2], 64, 0), mixed)]
    for first in (5, 9):
        low = jnp.where(lane < 32, move(fields[first], 32, 0), move(fields[first + 1], 32, 32))
        high = jnp.where(lane < 96, move(fields[first + 2], 32, 64), move(fields[first + 3], 32, 96))
        out.append(jnp.where(lane < 64, low, high))
    return out


def unpack_columns(packed, last):
    def move(x, width, at):
        end = 128 - width if last else 0
        return roll(x, end - at) if at != end else x

    out = [move(packed[0], 64, 0), move(packed[0], 64, 64), move(packed[1], 64, 0)]
    out += [move(packed[1], 32, 64), move(packed[1], 32, 96)]
    for t in (2, 3):
        out += [move(packed[t], 32, 32 * g) for g in range(4)]
    return out


def kernel(
    displace, load, history, stiffen, table, slope_hbm, basis_hbm, axial_hbm, cycle_hbm, modulus_hbm, radial_hbm,
    out_v,
    slope_ref, basis_ref, axial_ref, cycle_ref, modulus, radial,
    dext, hext, sext, load_v, table_v, pad_v, rsend, csend, rtop, rbot, cleft, cright, corner, stress_v,
    s1, r1, s2, r2, s3, r3, s4, r4,
    in_sem, table_sem, halo_send, halo_recv, a2a_send, a2a_recv, known,
):
    i = lax.axis_index("ax")
    j = lax.axis_index("circ")
    up_i, down_i = lax.rem(i + NX - 1, NX), lax.rem(i + 1, NX)
    left_j, right_j = lax.rem(j + NJ - 1, NJ), lax.rem(j + 1, NJ)

    own = [
        pltpu.make_async_copy(displace, dext.at[:, 8:40, 128:640], in_sem.at[0]),
        pltpu.make_async_copy(history, hext.at[:, 8:40, 128:640], in_sem.at[1]),
        pltpu.make_async_copy(stiffen, sext.at[8:40, 128:640], in_sem.at[2]),
        pltpu.make_async_copy(slope_hbm, slope_ref, in_sem.at[3]),
        pltpu.make_async_copy(basis_hbm, basis_ref, in_sem.at[4]),
        pltpu.make_async_copy(axial_hbm, axial_ref, in_sem.at[5]),
        pltpu.make_async_copy(cycle_hbm, cycle_ref, in_sem.at[6]),
        pltpu.make_async_copy(modulus_hbm, modulus, in_sem.at[7]),
        pltpu.make_async_copy(radial_hbm, radial, in_sem.at[8]),
        pltpu.make_async_copy(load, load_v, in_sem.at[9]),
    ]
    for copy in own:
        copy.start()
    table_copies = [pltpu.make_async_copy(table.at[k], table_v.at[k], table_sem.at[k]) for k in range(4)]

    barrier = pltpu.get_barrier_semaphore()

    def near_z(side, step):
        y_lo, z, core = lax.div(j, 16), lax.rem(lax.div(j, 2), 8), lax.rem(j, 2)
        y_lo = lax.rem(y_lo + side // 2, 2)
        core = lax.rem(core + side % 2, 2)
        return y_lo * 16 + lax.rem(z + step, 8) * 2 + core

    def signal(sem, di, dj):
        pl.semaphore_signal(sem, inc=1, device_id=(di, dj), device_id_type=MESH)

    for di in (up_i, down_i):
        for dj in (left_j, right_j, j):
            signal(barrier, di, dj)
    for side in range(4):
        for step in (7, 1, 0):
            if side or step:
                signal(barrier, i, near_z(side, step))
    for copy in table_copies:
        copy.start()

    for copy in own[:3]:
        copy.wait()
    for side, (d0, h0) in enumerate(((8, 8), (38, 39))):
        for p in range(3):
            rsend[side, 2 * p : 2 * p + 2, :] = dext[p, d0 : d0 + 2, 128:640]
        for n in range(9):
            rsend[side, 6 + n : 7 + n, :] = hext[n, h0 : h0 + 1, 128:640]
        rsend[side, 15:16, :] = sext[h0 : h0 + 1, 128:640]

    for side, cols in enumerate((slice(128, 256), slice(512, 640))):
        edge = [dext[p, 8:40, cols] for p in range(3)] + [hext[n, 8:40, cols] for n in range(9)] + [sext[8:40, cols]]
        for t, value in enumerate(pack_columns(edge, side == 1)):
            csend[side, t] = value

    pl.semaphore_wait(barrier, 17)

    copies = []

    def send(src, dst, device):
        k = len(copies)
        copy = pltpu.make_async_remote_copy(
            src_ref=src, dst_ref=dst, send_sem=halo_send.at[k], recv_sem=halo_recv.at[k],
            device_id=device, device_id_type=MESH,
        )
        copy.start()
        copies.append(copy)

    send(rsend.at[1], rtop, (down_i, j))
    send(rsend.at[0], rbot, (up_i, j))
    send(csend.at[1], cleft, (i, right_j))
    send(csend.at[0], cright, (i, left_j))
    send(rsend.at[1, :, 384:512], corner.at[0, 0], (down_i, right_j))
    send(rsend.at[1, :, 0:128], corner.at[0, 1], (down_i, left_j))
    send(rsend.at[0, :, 384:512], corner.at[1, 0], (up_i, right_j))
    send(rsend.at[0, :, 0:128], corner.at[1, 1], (up_i, left_j))

    def tell_z(k, step):
        for way in (step, 8 - step):
            signal(known.at[k], i, near_z(0, way))

    def tell_ax(k, step):
        for way in (step, NX - step):
            signal(known.at[k], lax.rem(i + way, NX), j)

    def hear(k):
        pl.semaphore_wait(known.at[k], 2)

    tell_z(0, 1)
    tell_ax(2, 1)
    for copy in own[3:]:
        copy.wait()
    pad_v[...] = jnp.zeros_like(pad_v)
    pad_v[0, :, 0:32] = slope_ref[...]
    pad_v[1, :, 0:32] = basis_ref[...]
    slope = block_diag(pad_v[0])
    slope_t = slope.T
    basis_t = block_diag(pad_v[1]).T
    slope, slope_t, basis_t = parts_of(slope), parts_of(slope_t), parts_of(basis_t)
    lane = lax.broadcasted_iota(jnp.int32, (32, NC), 1)
    row = lax.broadcasted_iota(jnp.int32, (32, NC), 0)
    picked = jnp.where(lane == row + 32 * i, jnp.broadcast_to(cycle_ref[...], (32, NC)), 0.0)
    denom = axial_ref[...] + jnp.sum(picked, axis=1, keepdims=True) + radial[j]

    hear(0)
    tell_z(1, 2)
    hear(2)
    tell_ax(3, 2)
    for copy in copies:
        copy.wait_recv()
    not_first, not_last = i > 0, i < NX - 1
    for ref, cols, left in ((cleft, slice(0, 128), True), (cright, slice(640, 768), False)):
        fields = unpack_columns([ref[t] for t in range(4)], left)
        for p in range(3):
            dext[p, 8:40, cols] = fields[p]
        for n in range(9):
            hext[n, 8:40, cols] = fields[3 + n]
        sext[8:40, cols] = fields[12]
    for side, (ref, d0, h0, there) in enumerate(((rtop, 6, 7, not_first), (rbot, 40, 40, not_last))):
        whole = jnp.concatenate([corner[side, 0], ref[...], corner[side, 1]], axis=1)
        whole = jnp.where(there, whole, 0.0)
        for p in range(3):
            dext[p, d0 : d0 + 2, :] = whole[2 * p : 2 * p + 2]
        for n in range(9):
            hext[n, h0 : h0 + 1, :] = whole[6 + n : 7 + n]
        sext[h0 : h0 + 1, :] = whole[15:16]

    windows = [(dext[p, 6:46, :], dext[p, 7:47, :], dext[p, 8:48, :]) for p in range(3)]
    grads = gradients(windows, slope_t)
    inside = lax.broadcasted_iota(jnp.int32, (40, 128), 0)
    keep = ((inside > 0) | not_first) & ((inside < 33) | not_last)
    for t in range(6):
        cols = slice(128 * t, 128 * (t + 1))
        piece = [g[:, cols] for g in grads]
        factor = 1.0 + sext[7:47, cols]
        for m in range(9):
            total = modulus[m, 0] * piece[0]
            for n in range(1, 9):
                total = total + modulus[m, n] * piece[n]
            stress_v[m, :, cols] = jnp.where(keep, factor * total + hext[m, 7:47, cols], 0.0)

    def stress(m):
        return stress_v[m, 0:32, :], stress_v[m, 1:33, :], stress_v[m, 2:34, :]

    y_hi, x = lax.div(i, 4), lax.rem(i, 4)
    y_lo, z, core = lax.div(j, 16), lax.rem(lax.div(j, 2), 8), lax.rem(j, 2)
    at_y = [16 * lax.rem(y_lo + dy, 2) for dy in range(2)]
    at_z = [2 * lax.rem(z + dz, 8) for dz in range(8)]
    at_core = [lax.rem(core + dc, 2) for dc in range(2)]
    at_y_hi = [4 * lax.rem(y_hi + dy, 4) for dy in range(4)]
    at_x = [lax.rem(x + dx, 4) for dx in range(4)]
    far_circ = [at_y[dy] + at_z[dz] + at_core[dc] for dz in (4, 3, 5, 2, 6, 1, 7, 0) for dy in (1, 0) for dc in (1, 0)][:-1]
    far_ax = [at_y_hi[dy] + at_x[dx] for dy in (2, 1, 3, 0) for dx in (2, 1, 3, 0)][:-1]

    def start(k, p, src, dst, on_circ):
        me = j if on_circ else i
        for d in far_circ if on_circ else far_ax:
            pltpu.make_async_remote_copy(
                src_ref=src.at[p, d], dst_ref=dst.at[p, me], send_sem=a2a_send.at[k], recv_sem=a2a_recv.at[k, p],
                device_id=(i, d) if on_circ else (d, j), device_id_type=MESH,
            ).start()
        pltpu.make_async_copy(src.at[p, me], dst.at[p, me], a2a_recv.at[k, p]).start()

    def arrived(k, p, dst):
        pltpu.make_async_copy(dst.at[p], dst.at[p], a2a_recv.at[k, p]).wait()

    for p in range(3):
        near, far = pulled(load_v[p], stress, p)
        mixed = dot3_t(*basis_t, near - dot3(far, *slope))
        for cl in range(4):
            s1[p, :, cl, :] = mixed[32 * cl : 32 * cl + 32]
        if p == 0:
            hear(1)
        start(0, p, s1, r1, True)

    hear(3)
    tell_ax(4, 4)
    table_copies[0].wait()
    for p in range(3):
        arrived(0, p, r1)
        line = jnp.concatenate([r1[p, :, cl, :] for cl in range(4)], axis=0)
        for it, four in enumerate(cycle_forward(line, table_v[0, 0], table_v[0, 1])):
            for i4 in range(4):
                s2[p, 4 * it + i4] = four[i4]
        if p == 0:
            hear(4)
        start(1, p, s2, r2, False)

    table_copies[1].wait()
    table_copies[2].wait()
    for p in range(3):
        arrived(1, p, r2)
        line = r2[p].reshape(128, 128)
        solved = axial_solve(line, denom, (table_v[1, 0], table_v[1, 1]), (table_v[2, 0], table_v[2, 1]))
        s3[p] = solved.reshape(NX, 8, 128)
        start(2, p, s3, r3, False)

    table_copies[3].wait()
    for p in range(3):
        arrived(2, p, r3)
        blocks = [[r3[p, 4 * it + i4] for i4 in range(4)] for it in range(4)]
        y = cycle_inverse(blocks, table_v[3, 0], table_v[3, 1])
        for c4 in range(4):
            s4[p, :, c4, :] = y[:, 128 * c4 : 128 * (c4 + 1)]
        start(3, p, s4, r4, True)

    for p in range(3):
        arrived(3, p, r4)
        line = jnp.concatenate([r4[p, :, c4, :] for c4 in range(4)], axis=0)
        out_v[128 * p : 128 * (p + 1), :] = dot3(line.T, *basis_t)

    for copy in copies:
        copy.wait_send()
    for k, (ref, count) in enumerate(((s1, NJ), (s2, NX), (s3, NX), (s4, NJ))):
        sent = ref.at[:, pl.ds(0, count - 1)]
        pltpu.make_async_copy(sent, sent, a2a_send.at[k]).wait()


def solution(mesh):
    table = tables()

    def body(displace, load, history, stiffen, modulus, slope, basis, axial, cycle, radial):
        hbm = pl.BlockSpec(memory_space=pltpu.HBM)
        dma = pltpu.SemaphoreType.DMA
        out = pl.pallas_call(
            kernel,
            out_shape=pltpu.VMEM((384, 128), F32),
            in_specs=[hbm] * 11,
            out_specs=pl.BlockSpec(memory_space=pltpu.VMEM),
            scratch_shapes=[
                pltpu.VMEM((R, R), F32),
                pltpu.VMEM((R, R), F32),
                pltpu.VMEM((1, NA), F32),
                pltpu.VMEM((1, NC), F32),
                pltpu.SMEM((9, 9), F32),
                pltpu.SMEM((R,), F32),
                pltpu.VMEM((3, 48, 768), F32),
                pltpu.VMEM((9, 48, 768), F32),
                pltpu.VMEM((48, 768), F32),
                pltpu.VMEM((3, 32, 512), F32),
                pltpu.VMEM((4, 2, 512, 512), BF16),
                pltpu.VMEM((2, 32, 128), F32),
                pltpu.VMEM((2, 16, 512), F32),
                pltpu.VMEM((2, 4, 32, 128), F32),
                pltpu.VMEM((16, 512), F32),
                pltpu.VMEM((16, 512), F32),
                pltpu.VMEM((4, 32, 128), F32),
                pltpu.VMEM((4, 32, 128), F32),
                pltpu.VMEM((2, 2, 16, 128), F32),
                pltpu.VMEM((9, 40, 768), F32),
                pltpu.VMEM((3, NJ, 4, 128), F32),
                pltpu.VMEM((3, NJ, 4, 128), F32),
                pltpu.VMEM((3, NX, 8, 128), F32),
                pltpu.VMEM((3, NX, 8, 128), F32),
                pltpu.VMEM((3, NX, 8, 128), F32),
                pltpu.VMEM((3, NX, 8, 128), F32),
                pltpu.VMEM((3, NJ, 4, 128), F32),
                pltpu.VMEM((3, NJ, 4, 128), F32),
                dma((10,)),
                dma((4,)),
                dma((8,)),
                dma((8,)),
                dma((4,)),
                dma((4, 3)),
                pltpu.SemaphoreType.REGULAR((5,)),
            ],
            compiler_params=pltpu.CompilerParams(
                collective_id=0, has_side_effects=True, vmem_limit_bytes=60 * 1024 * 1024
            ),
        )(
            displace, load, history, stiffen, jnp.asarray(table), slope, basis,
            axial.reshape(1, NA), cycle.reshape(1, NC), modulus, radial,
        )
        return out.reshape(3, 1, NC * R)

    return jax.shard_map(
        body,
        mesh=mesh,
        in_specs=(
            P(None, "ax", "circ"),
            P(None, "ax", "circ"),
            P(None, "ax", "circ"),
            P("ax", "circ"),
            P(),
            P(),
            P(),
            P(),
            P(),
            P(),
        ),
        out_specs=P(None, ("ax", "circ"), None),
        check_vma=False,
    )
```

```python
import math

import jax
import jax.numpy as jnp
import ml_dtypes
import numpy as np
from jax import lax
from jax.experimental import pallas as pl
from jax.experimental.pallas import tpu as pltpu
from jax.sharding import PartitionSpec as P

NA = 512
NC = 512
R = 32
NX = 16
NJ = 32
F32 = jnp.float32
BF16 = jnp.bfloat16
MESH = pl.DeviceIdType.MESH


def cycle_table():
    col = np.arange(NC)[:, None]
    mode = np.arange(NC)[None, :]
    half = NC // 2
    folded = np.where(mode <= half, mode, mode - half)
    shift = np.where(mode <= half, 0.0, 0.5 * np.pi)
    scale = np.where((mode == 0) | (mode == half), math.sqrt(1.0 / NC), math.sqrt(2.0 / NC))
    return np.cos((col * folded % NC) * (2.0 * np.pi / NC) - shift) * scale


def axial_table():
    first = (np.arange(NA) + 1)[:, None]
    mode = (np.arange(NA) + 1)[None, :]
    return np.sin((first * mode % (2 * (NA + 1))) * (np.pi / (NA + 1))) * math.sqrt(2.0 / (NA + 1))


def two_parts(table):
    table = table.astype(np.float32)
    high = table.astype(ml_dtypes.bfloat16)
    low = (table - high.astype(np.float32)).astype(ml_dtypes.bfloat16)
    return np.stack([high, low])


def tables():
    cyc, axi = cycle_table(), axial_table()
    q, cl, j = np.meshgrid(np.arange(4), np.arange(4), np.arange(NJ), indexing="ij")
    cycle_in = cyc[(16 * j + 4 * q + cl).reshape(-1)]
    a4, i, ah = np.meshgrid(np.arange(4), np.arange(NX), np.arange(8), indexing="ij")
    perm = (32 * i + 8 * a4 + ah).reshape(-1)
    c4, cg = np.meshgrid(np.arange(4), np.arange(128), indexing="ij")
    cycle_out = cyc.T[:, (4 * cg + c4).reshape(-1)]
    return np.stack([two_parts(cycle_in), two_parts(axi[perm]), two_parts(axi[:, perm]), two_parts(cycle_out)])


def roll(x, shift):
    return pltpu.roll(x, shift % x.shape[-1], x.ndim - 1)


def parts_of(x):
    high = x.astype(BF16)
    return high, (x - high.astype(F32)).astype(BF16)


def mm(a, b):
    return jnp.dot(a, b, preferred_element_type=F32)


def mm_t(a, b):
    return lax.dot_general(a, b, (((1,), (1,)), ((), ())), preferred_element_type=F32)


def dot3(x, high, low):
    xh, xl = parts_of(x)
    n = x.shape[0]
    both = mm(jnp.concatenate([xh, xl], axis=0), high)
    return both[:n] + (both[n:] + mm(xh, low))


def dot3_t(high, low, x):
    xh, xl = parts_of(x)
    n = high.shape[0]
    both = mm_t(jnp.concatenate([high, low], axis=0), xh)
    return both[:n] + (both[n:] + mm_t(high, xl))


def block_diag(x):
    wide = x + roll(x, 32)
    wide = wide + roll(wide, 64)
    full = jnp.concatenate([wide] * 4, axis=0)
    row = lax.broadcasted_iota(jnp.int32, (128, 128), 0) // 32
    lane = lax.broadcasted_iota(jnp.int32, (128, 128), 1) // 32
    return jnp.where(row == lane, full, 0.0)


def swap_groups(v):
    group = lax.broadcasted_iota(jnp.int32, v[0].shape, 1) // 32
    low_half = group < 2
    a0 = jnp.where(low_half, v[0], roll(v[2], 64))
    a2 = jnp.where(low_half, roll(v[0], 64), v[2])
    a1 = jnp.where(low_half, v[1], roll(v[3], 64))
    a3 = jnp.where(low_half, roll(v[1], 64), v[3])
    even = (group % 2) == 0
    u0 = jnp.where(even, a0, roll(a1, 32))
    u1 = jnp.where(even, roll(a0, -32), a1)
    u2 = jnp.where(even, a2, roll(a3, 32))
    u3 = jnp.where(even, roll(a2, -32), a3)
    return [u0, u1, u2, u3]


def tiles(x):
    return [x[:, 128 * t : 128 * (t + 1)] for t in range(x.shape[1] // 128)]


def rows(x, n):
    return [x[n * t : n * (t + 1)] for t in range(x.shape[0] // n)]


def smooth_a(up, mid, down):
    return (up + 4.0 * mid + down) * (1.0 / 6.0)


def slope_a(up, down):
    return (down - up) * 0.5


def smooth_c(x):
    return (roll(x, 32) + 4.0 * x + roll(x, -32)) * (1.0 / 6.0)


def slope_c(x):
    return (roll(x, -32) - roll(x, 32)) * 0.5


def gradients(windows, slope_t):
    first, second, plain = [], [], []
    for up, mid, down in windows:
        first.append(smooth_c(slope_a(up, down)))
        smooth = smooth_a(up, mid, down)
        second.append(slope_c(smooth))
        plain.append(smooth_c(smooth))
    stacked = jnp.concatenate([t for x in plain for t in tiles(x)], axis=0)
    mixed = rows(dot3(stacked, *slope_t), 40)
    third = [jnp.concatenate(mixed[6 * p : 6 * p + 6], axis=1) for p in range(3)]
    return first + second + third


def pulled(load, stress, p):
    up, _, down = stress(p)
    part = smooth_c(slope_a(up, down))
    part = part + slope_c(smooth_a(*stress(3 + p)))
    third = smooth_c(smooth_a(*stress(6 + p)))
    near = load + part[:, 128:640]
    return jnp.concatenate(tiles(near), axis=0), jnp.concatenate(tiles(third[:, 128:640]), axis=0)


def cycle_forward(x, high, low):
    y = dot3(jnp.concatenate(rows(x.T, 32), axis=1), high, low)
    return [swap_groups(rows(t, 8)) for t in tiles(y)]


def axial_solve(x, weight, forward, inverse):
    modes = dot3(jnp.concatenate(rows(x.T, 32), axis=1), *forward)
    y = dot3(modes * weight, *inverse)
    return jnp.concatenate(tiles(y), axis=0).T


def cycle_inverse(blocks, high, low):
    cols = [jnp.concatenate(swap_groups(four), axis=0) for four in blocks]
    return dot3(jnp.concatenate(cols, axis=1), high, low)


def pack_columns(fields, last):
    lane = lax.broadcasted_iota(jnp.int32, (32, 128), 1)

    def move(x, width, at):
        start = 128 - width if last else 0
        return roll(x, at - start) if at != start else x

    two = jnp.where(lane < 64, move(fields[0], 64, 0), move(fields[1], 64, 64))
    mixed = jnp.where(lane < 96, move(fields[3], 32, 64), move(fields[4], 32, 96))
    out = [two, jnp.where(lane < 64, move(fields[2], 64, 0), mixed)]
    for first in (5, 9):
        low = jnp.where(lane < 32, move(fields[first], 32, 0), move(fields[first + 1], 32, 32))
        high = jnp.where(lane < 96, move(fields[first + 2], 32, 64), move(fields[first + 3], 32, 96))
        out.append(jnp.where(lane < 64, low, high))
    return out


def unpack_columns(packed, last):
    def move(x, width, at):
        end = 128 - width if last else 0
        return roll(x, end - at) if at != end else x

    out = [move(packed[0], 64, 0), move(packed[0], 64, 64), move(packed[1], 64, 0)]
    out += [move(packed[1], 32, 64), move(packed[1], 32, 96)]
    for t in (2, 3):
        out += [move(packed[t], 32, 32 * g) for g in range(4)]
    return out


def kernel(
    displace, load, history, stiffen, table, slope_hbm, basis_hbm, axial_hbm, cycle_hbm, modulus_hbm, radial_hbm,
    out_v,
    slope_ref, basis_ref, axial_ref, cycle_ref, modulus, radial,
    dext, hext, sext, load_v, table_v, pad_v, rsend, csend, rtop, rbot, cleft, cright, corner, stress_v,
    s1, r1, s2, r2, s3, r3, s4, r4,
    in_sem, table_sem, halo_send, halo_recv, a2a_send, a2a_recv, known,
):
    i = lax.axis_index("ax")
    j = lax.axis_index("circ")
    up_i, down_i = lax.rem(i + NX - 1, NX), lax.rem(i + 1, NX)
    left_j, right_j = lax.rem(j + NJ - 1, NJ), lax.rem(j + 1, NJ)

    own = [
        pltpu.make_async_copy(displace, dext.at[:, 8:40, 128:640], in_sem.at[0]),
        pltpu.make_async_copy(history, hext.at[:, 8:40, 128:640], in_sem.at[1]),
        pltpu.make_async_copy(stiffen, sext.at[8:40, 128:640], in_sem.at[2]),
        pltpu.make_async_copy(slope_hbm, slope_ref, in_sem.at[3]),
        pltpu.make_async_copy(basis_hbm, basis_ref, in_sem.at[4]),
        pltpu.make_async_copy(axial_hbm, axial_ref, in_sem.at[5]),
        pltpu.make_async_copy(cycle_hbm, cycle_ref, in_sem.at[6]),
        pltpu.make_async_copy(modulus_hbm, modulus, in_sem.at[7]),
        pltpu.make_async_copy(radial_hbm, radial, in_sem.at[8]),
        pltpu.make_async_copy(load, load_v, in_sem.at[9]),
    ]
    for copy in own:
        copy.start()
    table_copies = [pltpu.make_async_copy(table.at[k], table_v.at[k], table_sem.at[k]) for k in range(4)]

    barrier = pltpu.get_barrier_semaphore()

    def near_z(side, step):
        y_lo, z, core = lax.div(j, 16), lax.rem(lax.div(j, 2), 8), lax.rem(j, 2)
        y_lo = lax.rem(y_lo + side // 2, 2)
        core = lax.rem(core + side % 2, 2)
        return y_lo * 16 + lax.rem(z + step, 8) * 2 + core

    def signal(sem, di, dj):
        pl.semaphore_signal(sem, inc=1, device_id=(di, dj), device_id_type=MESH)

    for di in (up_i, down_i):
        for dj in (left_j, right_j, j):
            signal(barrier, di, dj)
    for side in range(4):
        for step in (7, 1, 0):
            if side or step:
                signal(barrier, i, near_z(side, step))
    for copy in table_copies:
        copy.start()

    for copy in own[:3]:
        copy.wait()
    for side, (d0, h0) in enumerate(((8, 8), (38, 39))):
        for p in range(3):
            rsend[side, 2 * p : 2 * p + 2, :] = dext[p, d0 : d0 + 2, 128:640]
        for n in range(9):
            rsend[side, 6 + n : 7 + n, :] = hext[n, h0 : h0 + 1, 128:640]
        rsend[side, 15:16, :] = sext[h0 : h0 + 1, 128:640]

    for side, cols in enumerate((slice(128, 256), slice(512, 640))):
        edge = [dext[p, 8:40, cols] for p in range(3)] + [hext[n, 8:40, cols] for n in range(9)] + [sext[8:40, cols]]
        for t, value in enumerate(pack_columns(edge, side == 1)):
            csend[side, t] = value

    pl.semaphore_wait(barrier, 17)

    copies = []

    def send(src, dst, device):
        k = len(copies)
        copy = pltpu.make_async_remote_copy(
            src_ref=src, dst_ref=dst, send_sem=halo_send.at[k], recv_sem=halo_recv.at[k],
            device_id=device, device_id_type=MESH,
        )
        copy.start()
        copies.append(copy)

    send(rsend.at[1], rtop, (down_i, j))
    send(rsend.at[0], rbot, (up_i, j))
    send(csend.at[1], cleft, (i, right_j))
    send(csend.at[0], cright, (i, left_j))
    send(rsend.at[1, :, 384:512], corner.at[0, 0], (down_i, right_j))
    send(rsend.at[1, :, 0:128], corner.at[0, 1], (down_i, left_j))
    send(rsend.at[0, :, 384:512], corner.at[1, 0], (up_i, right_j))
    send(rsend.at[0, :, 0:128], corner.at[1, 1], (up_i, left_j))

    def tell_z(k, step):
        for way in (step, 8 - step):
            signal(known.at[k], i, near_z(0, way))

    def tell_ax(k, step):
        for way in (step, NX - step):
            signal(known.at[k], lax.rem(i + way, NX), j)

    def hear(k):
        pl.semaphore_wait(known.at[k], 2)

    tell_z(0, 1)
    tell_ax(2, 1)
    for copy in own[3:]:
        copy.wait()
    pad_v[...] = jnp.zeros_like(pad_v)
    pad_v[0, :, 0:32] = slope_ref[...]
    pad_v[1, :, 0:32] = basis_ref[...]
    slope = block_diag(pad_v[0])
    slope_t = slope.T
    basis_t = block_diag(pad_v[1]).T
    slope, slope_t, basis_t = parts_of(slope), parts_of(slope_t), parts_of(basis_t)
    lane = lax.broadcasted_iota(jnp.int32, (32, NC), 1)
    row = lax.broadcasted_iota(jnp.int32, (32, NC), 0)
    picked = jnp.where(lane == row + 32 * i, jnp.broadcast_to(cycle_ref[...], (32, NC)), 0.0)
    weight = 1.0 / (axial_ref[...] + jnp.sum(picked, axis=1, keepdims=True) + radial[j])

    hear(0)
    tell_z(1, 2)
    hear(2)
    tell_ax(3, 2)
    for copy in copies:
        copy.wait_recv()
    not_first, not_last = i > 0, i < NX - 1
    for ref, cols, left in ((cleft, slice(0, 128), True), (cright, slice(640, 768), False)):
        fields = unpack_columns([ref[t] for t in range(4)], left)
        for p in range(3):
            dext[p, 8:40, cols] = fields[p]
        for n in range(9):
            hext[n, 8:40, cols] = fields[3 + n]
        sext[8:40, cols] = fields[12]
    for side, (ref, d0, h0, there) in enumerate(((rtop, 6, 7, not_first), (rbot, 40, 40, not_last))):
        whole = jnp.concatenate([corner[side, 0], ref[...], corner[side, 1]], axis=1)
        whole = jnp.where(there, whole, 0.0)
        for p in range(3):
            dext[p, d0 : d0 + 2, :] = whole[2 * p : 2 * p + 2]
        for n in range(9):
            hext[n, h0 : h0 + 1, :] = whole[6 + n : 7 + n]
        sext[h0 : h0 + 1, :] = whole[15:16]

    windows = [(dext[p, 6:46, :], dext[p, 7:47, :], dext[p, 8:48, :]) for p in range(3)]
    grads = gradients(windows, slope_t)
    inside = lax.broadcasted_iota(jnp.int32, (40, 128), 0)
    keep = ((inside > 0) | not_first) & ((inside < 33) | not_last)
    factor = [1.0 + sext[7:47, 128 * t : 128 * (t + 1)] for t in range(6)]

    def couple(m):
        for t in range(6):
            cols = slice(128 * t, 128 * (t + 1))
            total = modulus[m, 0] * grads[0][:, cols]
            for n in range(1, 9):
                total = total + modulus[m, n] * grads[n][:, cols]
            stress_v[m, :, cols] = jnp.where(keep, factor[t] * total + hext[m, 7:47, cols], 0.0)

    def stress(m):
        return stress_v[m, 0:32, :], stress_v[m, 1:33, :], stress_v[m, 2:34, :]

    y_hi, x = lax.div(i, 4), lax.rem(i, 4)
    y_lo, z, core = lax.div(j, 16), lax.rem(lax.div(j, 2), 8), lax.rem(j, 2)
    at_y = [16 * lax.rem(y_lo + dy, 2) for dy in range(2)]
    at_z = [2 * lax.rem(z + dz, 8) for dz in range(8)]
    at_core = [lax.rem(core + dc, 2) for dc in range(2)]
    at_y_hi = [4 * lax.rem(y_hi + dy, 4) for dy in range(4)]
    at_x = [lax.rem(x + dx, 4) for dx in range(4)]
    far_circ = [at_y[dy] + at_z[dz] + at_core[dc] for dz in (4, 3, 5, 2, 6, 1, 7, 0) for dy in (1, 0) for dc in (1, 0)][:-1]
    far_ax = [at_y_hi[dy] + at_x[dx] for dy in (2, 1, 3, 0) for dx in (2, 1, 3, 0)][:-1]

    def start(k, p, src, dst, on_circ):
        me = j if on_circ else i
        for d in far_circ if on_circ else far_ax:
            pltpu.make_async_remote_copy(
                src_ref=src.at[p, d], dst_ref=dst.at[p, me], send_sem=a2a_send.at[k], recv_sem=a2a_recv.at[k, p],
                device_id=(i, d) if on_circ else (d, j), device_id_type=MESH,
            ).start()
        pltpu.make_async_copy(src.at[p, me], dst.at[p, me], a2a_recv.at[k, p]).start()

    def arrived(k, p, dst):
        pltpu.make_async_copy(dst.at[p], dst.at[p], a2a_recv.at[k, p]).wait()

    for p in range(3):
        for m in (p, 3 + p, 6 + p):
            couple(m)
        near, far = pulled(load_v[p], stress, p)
        mixed = dot3_t(*basis_t, near - dot3(far, *slope))
        for cl in range(4):
            s1[p, :, cl, :] = mixed[32 * cl : 32 * cl + 32]
        if p == 0:
            hear(1)
        start(0, p, s1, r1, True)

    hear(3)
    tell_ax(4, 4)
    table_copies[0].wait()
    for p in range(3):
        arrived(0, p, r1)
        line = jnp.concatenate([r1[p, :, cl, :] for cl in range(4)], axis=0)
        for it, four in enumerate(cycle_forward(line, table_v[0, 0], table_v[0, 1])):
            for i4 in range(4):
                s2[p, 4 * it + i4] = four[i4]
        if p == 0:
            hear(4)
        start(1, p, s2, r2, False)

    table_copies[1].wait()
    table_copies[2].wait()
    for p in range(3):
        arrived(1, p, r2)
        line = r2[p].reshape(128, 128)
        solved = axial_solve(line, weight, (table_v[1, 0], table_v[1, 1]), (table_v[2, 0], table_v[2, 1]))
        s3[p] = solved.reshape(NX, 8, 128)
        start(2, p, s3, r3, False)

    table_copies[3].wait()
    for p in range(3):
        arrived(2, p, r3)
        blocks = [[r3[p, 4 * it + i4] for i4 in range(4)] for it in range(4)]
        y = cycle_inverse(blocks, table_v[3, 0], table_v[3, 1])
        for c4 in range(4):
            s4[p, :, c4, :] = y[:, 128 * c4 : 128 * (c4 + 1)]
        start(3, p, s4, r4, True)

    for p in range(3):
        arrived(3, p, r4)
        line = jnp.concatenate([r4[p, :, c4, :] for c4 in range(4)], axis=0)
        out_v[128 * p : 128 * (p + 1), :] = dot3(line.T, *basis_t)

    for copy in copies:
        copy.wait_send()
    for k, (ref, count) in enumerate(((s1, NJ), (s2, NX), (s3, NX), (s4, NJ))):
        sent = ref.at[:, pl.ds(0, count - 1)]
        pltpu.make_async_copy(sent, sent, a2a_send.at[k]).wait()


def solution(mesh):
    table = tables()

    def body(displace, load, history, stiffen, modulus, slope, basis, axial, cycle, radial):
        hbm = pl.BlockSpec(memory_space=pltpu.HBM)
        dma = pltpu.SemaphoreType.DMA
        out = pl.pallas_call(
            kernel,
            out_shape=pltpu.VMEM((384, 128), F32),
            in_specs=[hbm] * 11,
            out_specs=pl.BlockSpec(memory_space=pltpu.VMEM),
            scratch_shapes=[
                pltpu.VMEM((R, R), F32),
                pltpu.VMEM((R, R), F32),
                pltpu.VMEM((1, NA), F32),
                pltpu.VMEM((1, NC), F32),
                pltpu.SMEM((9, 9), F32),
                pltpu.SMEM((R,), F32),
                pltpu.VMEM((3, 48, 768), F32),
                pltpu.VMEM((9, 48, 768), F32),
                pltpu.VMEM((48, 768), F32),
                pltpu.VMEM((3, 32, 512), F32),
                pltpu.VMEM((4, 2, 512, 512), BF16),
                pltpu.VMEM((2, 32, 128), F32),
                pltpu.VMEM((2, 16, 512), F32),
                pltpu.VMEM((2, 4, 32, 128), F32),
                pltpu.VMEM((16, 512), F32),
                pltpu.VMEM((16, 512), F32),
                pltpu.VMEM((4, 32, 128), F32),
                pltpu.VMEM((4, 32, 128), F32),
                pltpu.VMEM((2, 2, 16, 128), F32),
                pltpu.VMEM((9, 40, 768), F32),
                pltpu.VMEM((3, NJ, 4, 128), F32),
                pltpu.VMEM((3, NJ, 4, 128), F32),
                pltpu.VMEM((3, NX, 8, 128), F32),
                pltpu.VMEM((3, NX, 8, 128), F32),
                pltpu.VMEM((3, NX, 8, 128), F32),
                pltpu.VMEM((3, NX, 8, 128), F32),
                pltpu.VMEM((3, NJ, 4, 128), F32),
                pltpu.VMEM((3, NJ, 4, 128), F32),
                dma((10,)),
                dma((4,)),
                dma((8,)),
                dma((8,)),
                dma((4,)),
                dma((4, 3)),
                pltpu.SemaphoreType.REGULAR((5,)),
            ],
            compiler_params=pltpu.CompilerParams(
                collective_id=0, has_side_effects=True, vmem_limit_bytes=60 * 1024 * 1024
            ),
        )(
            displace, load, history, stiffen, jnp.asarray(table), slope, basis,
            axial.reshape(1, NA), cycle.reshape(1, NC), modulus, radial,
        )
        return out.reshape(3, 1, NC * R)

    return jax.shard_map(
        body,
        mesh=mesh,
        in_specs=(
            P(None, "ax", "circ"),
            P(None, "ax", "circ"),
            P(None, "ax", "circ"),
            P("ax", "circ"),
            P(),
            P(),
            P(),
            P(),
            P(),
            P(),
        ),
        out_specs=P(None, ("ax", "circ"), None),
        check_vma=False,
    )
```

```python
import math

import jax
import jax.numpy as jnp
import ml_dtypes
import numpy as np
from jax import lax
from jax.experimental import pallas as pl
from jax.experimental.pallas import tpu as pltpu
from jax.sharding import PartitionSpec as P

NA = 512
NC = 512
R = 32
NX = 16
NJ = 32
F32 = jnp.float32
BF16 = jnp.bfloat16
MESH = pl.DeviceIdType.MESH


def cycle_table():
    col = np.arange(NC)[:, None]
    mode = np.arange(NC)[None, :]
    half = NC // 2
    folded = np.where(mode <= half, mode, mode - half)
    shift = np.where(mode <= half, 0.0, 0.5 * np.pi)
    scale = np.where((mode == 0) | (mode == half), math.sqrt(1.0 / NC), math.sqrt(2.0 / NC))
    return np.cos((col * folded % NC) * (2.0 * np.pi / NC) - shift) * scale


def axial_table():
    first = (np.arange(NA) + 1)[:, None]
    mode = (np.arange(NA) + 1)[None, :]
    return np.sin((first * mode % (2 * (NA + 1))) * (np.pi / (NA + 1))) * math.sqrt(2.0 / (NA + 1))


def two_parts(table):
    table = table.astype(np.float32)
    high = table.astype(ml_dtypes.bfloat16)
    low = (table - high.astype(np.float32)).astype(ml_dtypes.bfloat16)
    return np.stack([high, low])


def tables():
    cyc, axi = cycle_table(), axial_table()
    q, cl, j = np.meshgrid(np.arange(4), np.arange(4), np.arange(NJ), indexing="ij")
    cycle_in = cyc[(16 * j + 4 * q + cl).reshape(-1)]
    a4, i, ah = np.meshgrid(np.arange(4), np.arange(NX), np.arange(8), indexing="ij")
    perm = (32 * i + 8 * a4 + ah).reshape(-1)
    c4, cg = np.meshgrid(np.arange(4), np.arange(128), indexing="ij")
    cycle_out = cyc.T[:, (4 * cg + c4).reshape(-1)]
    return np.stack([two_parts(cycle_in), two_parts(axi[perm]), two_parts(axi[:, perm]), two_parts(cycle_out)])


def roll(x, shift):
    return pltpu.roll(x, shift % x.shape[-1], x.ndim - 1)


def parts_of(x):
    high = x.astype(BF16)
    return high, (x - high.astype(F32)).astype(BF16)


def mm(a, b):
    return jnp.dot(a, b, preferred_element_type=F32)


def mm_t(a, b):
    return lax.dot_general(a, b, (((1,), (1,)), ((), ())), preferred_element_type=F32)


def dot3(x, high, low):
    xh, xl = parts_of(x)
    n = x.shape[0]
    both = mm(jnp.concatenate([xh, xl], axis=0), high)
    return both[:n] + (both[n:] + mm(xh, low))


def dot3_t(high, low, x):
    xh, xl = parts_of(x)
    n = high.shape[0]
    both = mm_t(jnp.concatenate([high, low], axis=0), xh)
    return both[:n] + (both[n:] + mm_t(high, xl))


def block_diag(x):
    wide = x + roll(x, 32)
    wide = wide + roll(wide, 64)
    full = jnp.concatenate([wide] * 4, axis=0)
    row = lax.broadcasted_iota(jnp.int32, (128, 128), 0) // 32
    lane = lax.broadcasted_iota(jnp.int32, (128, 128), 1) // 32
    return jnp.where(row == lane, full, 0.0)


def swap_groups(v):
    group = lax.broadcasted_iota(jnp.int32, v[0].shape, 1) // 32
    low_half = group < 2
    a0 = jnp.where(low_half, v[0], roll(v[2], 64))
    a2 = jnp.where(low_half, roll(v[0], 64), v[2])
    a1 = jnp.where(low_half, v[1], roll(v[3], 64))
    a3 = jnp.where(low_half, roll(v[1], 64), v[3])
    even = (group % 2) == 0
    u0 = jnp.where(even, a0, roll(a1, 32))
    u1 = jnp.where(even, roll(a0, -32), a1)
    u2 = jnp.where(even, a2, roll(a3, 32))
    u3 = jnp.where(even, roll(a2, -32), a3)
    return [u0, u1, u2, u3]


def tiles(x):
    return [x[:, 128 * t : 128 * (t + 1)] for t in range(x.shape[1] // 128)]


def rows(x, n):
    return [x[n * t : n * (t + 1)] for t in range(x.shape[0] // n)]


def smooth_a(up, mid, down):
    return (up + 4.0 * mid + down) * (1.0 / 6.0)


def slope_a(up, down):
    return (down - up) * 0.5


def smooth_c(x):
    return (roll(x, 32) + 4.0 * x + roll(x, -32)) * (1.0 / 6.0)


def slope_c(x):
    return (roll(x, -32) - roll(x, 32)) * 0.5


def gradients(windows, slope_t):
    first, second, plain = [], [], []
    for up, mid, down in windows:
        first.append(smooth_c(slope_a(up, down)))
        smooth = smooth_a(up, mid, down)
        second.append(slope_c(smooth))
        plain.append(smooth_c(smooth))
    stacked = jnp.concatenate([t for x in plain for t in tiles(x)], axis=0)
    mixed = rows(dot3(stacked, *slope_t), 40)
    third = [jnp.concatenate(mixed[6 * p : 6 * p + 6], axis=1) for p in range(3)]
    return first + second + third


def pulled(load, stress, p):
    up, _, down = stress(p)
    part = smooth_c(slope_a(up, down))
    part = part + slope_c(smooth_a(*stress(3 + p)))
    third = smooth_c(smooth_a(*stress(6 + p)))
    near = load + part[:, 128:640]
    return jnp.concatenate(tiles(near), axis=0), jnp.concatenate(tiles(third[:, 128:640]), axis=0)


def cycle_forward(x, high, low):
    y = dot3(jnp.concatenate(rows(x.T, 32), axis=1), high, low)
    return [swap_groups(rows(t, 8)) for t in tiles(y)]


def axial_solve(x, weight, forward, inverse):
    modes = dot3(jnp.concatenate(rows(x.T, 32), axis=1), *forward)
    y = dot3(modes * weight, *inverse)
    return jnp.concatenate(tiles(y), axis=0).T


def cycle_inverse(blocks, high, low):
    cols = [jnp.concatenate(swap_groups(four), axis=0) for four in blocks]
    return dot3(jnp.concatenate(cols, axis=1), high, low)


def pack_columns(fields, last):
    lane = lax.broadcasted_iota(jnp.int32, (32, 128), 1)

    def move(x, width, at):
        start = 128 - width if last else 0
        return roll(x, at - start) if at != start else x

    two = jnp.where(lane < 64, move(fields[0], 64, 0), move(fields[1], 64, 64))
    mixed = jnp.where(lane < 96, move(fields[3], 32, 64), move(fields[4], 32, 96))
    out = [two, jnp.where(lane < 64, move(fields[2], 64, 0), mixed)]
    for first in (5, 9):
        low = jnp.where(lane < 32, move(fields[first], 32, 0), move(fields[first + 1], 32, 32))
        high = jnp.where(lane < 96, move(fields[first + 2], 32, 64), move(fields[first + 3], 32, 96))
        out.append(jnp.where(lane < 64, low, high))
    return out


def unpack_columns(packed, last):
    def move(x, width, at):
        end = 128 - width if last else 0
        return roll(x, end - at) if at != end else x

    out = [move(packed[0], 64, 0), move(packed[0], 64, 64), move(packed[1], 64, 0)]
    out += [move(packed[1], 32, 64), move(packed[1], 32, 96)]
    for t in (2, 3):
        out += [move(packed[t], 32, 32 * g) for g in range(4)]
    return out


def kernel(
    displace, load, history, stiffen, table, slope_hbm, basis_hbm, axial_hbm, cycle_hbm, modulus_hbm, radial_hbm,
    out_v,
    slope_ref, basis_ref, axial_ref, cycle_ref, modulus, radial,
    dext, hext, sext, load_v, table_v, pad_v, rsend, csend, rtop, rbot, cleft, cright, corner, stress_v,
    s1, r1, s2, r2, s3, r3, s4, r4,
    in_sem, table_sem, halo_send, halo_recv, a2a_send, a2a_recv, known,
):
    i = lax.axis_index("ax")
    j = lax.axis_index("circ")
    up_i, down_i = lax.rem(i + NX - 1, NX), lax.rem(i + 1, NX)
    left_j, right_j = lax.rem(j + NJ - 1, NJ), lax.rem(j + 1, NJ)

    own = [
        pltpu.make_async_copy(displace, dext.at[:, 8:40, 128:640], in_sem.at[0]),
        pltpu.make_async_copy(history, hext.at[:, 8:40, 128:640], in_sem.at[1]),
        pltpu.make_async_copy(stiffen, sext.at[8:40, 128:640], in_sem.at[2]),
        pltpu.make_async_copy(slope_hbm, slope_ref, in_sem.at[3]),
        pltpu.make_async_copy(basis_hbm, basis_ref, in_sem.at[4]),
        pltpu.make_async_copy(axial_hbm, axial_ref, in_sem.at[5]),
        pltpu.make_async_copy(cycle_hbm, cycle_ref, in_sem.at[6]),
        pltpu.make_async_copy(modulus_hbm, modulus, in_sem.at[7]),
        pltpu.make_async_copy(radial_hbm, radial, in_sem.at[8]),
        pltpu.make_async_copy(load, load_v, in_sem.at[9]),
    ]
    for copy in own:
        copy.start()
    table_copies = [pltpu.make_async_copy(table.at[k], table_v.at[k], table_sem.at[k]) for k in range(4)]

    barrier = pltpu.get_barrier_semaphore()

    def near_z(side, step):
        y_lo, z, core = lax.div(j, 16), lax.rem(lax.div(j, 2), 8), lax.rem(j, 2)
        y_lo = lax.rem(y_lo + side // 2, 2)
        core = lax.rem(core + side % 2, 2)
        return y_lo * 16 + lax.rem(z + step, 8) * 2 + core

    def signal(sem, di, dj):
        pl.semaphore_signal(sem, inc=1, device_id=(di, dj), device_id_type=MESH)

    for di in (up_i, down_i):
        for dj in (left_j, right_j, j):
            signal(barrier, di, dj)
    for side in range(4):
        for step in (7, 1, 0):
            if side or step:
                signal(barrier, i, near_z(side, step))
    for copy in table_copies:
        copy.start()

    for copy in own[:3]:
        copy.wait()
    for side, (d0, h0) in enumerate(((8, 8), (38, 39))):
        for p in range(3):
            rsend[side, 2 * p : 2 * p + 2, :] = dext[p, d0 : d0 + 2, 128:640]
        for n in range(9):
            rsend[side, 6 + n : 7 + n, :] = hext[n, h0 : h0 + 1, 128:640]
        rsend[side, 15:16, :] = sext[h0 : h0 + 1, 128:640]

    for side, cols in enumerate((slice(128, 256), slice(512, 640))):
        edge = [dext[p, 8:40, cols] for p in range(3)] + [hext[n, 8:40, cols] for n in range(9)] + [sext[8:40, cols]]
        for t, value in enumerate(pack_columns(edge, side == 1)):
            csend[side, t] = value

    pl.semaphore_wait(barrier, 17)

    copies = []

    def send(src, dst, device):
        k = len(copies)
        copy = pltpu.make_async_remote_copy(
            src_ref=src, dst_ref=dst, send_sem=halo_send.at[k], recv_sem=halo_recv.at[k],
            device_id=device, device_id_type=MESH,
        )
        copy.start()
        copies.append(copy)

    send(rsend.at[1, :, 384:512], corner.at[0, 0], (down_i, right_j))
    send(rsend.at[1, :, 0:128], corner.at[0, 1], (down_i, left_j))
    send(rsend.at[0, :, 384:512], corner.at[1, 0], (up_i, right_j))
    send(rsend.at[0, :, 0:128], corner.at[1, 1], (up_i, left_j))
    send(rsend.at[1], rtop, (down_i, j))
    send(rsend.at[0], rbot, (up_i, j))
    send(csend.at[1], cleft, (i, right_j))
    send(csend.at[0], cright, (i, left_j))

    def tell_z(k, step):
        for way in (step, 8 - step):
            signal(known.at[k], i, near_z(0, way))

    def tell_ax(k, step):
        for way in (step, NX - step):
            signal(known.at[k], lax.rem(i + way, NX), j)

    def hear(k):
        pl.semaphore_wait(known.at[k], 2)

    tell_z(0, 1)
    tell_ax(2, 1)
    for copy in own[3:]:
        copy.wait()
    pad_v[...] = jnp.zeros_like(pad_v)
    pad_v[0, :, 0:32] = slope_ref[...]
    pad_v[1, :, 0:32] = basis_ref[...]
    slope = block_diag(pad_v[0])
    slope_t = slope.T
    basis_t = block_diag(pad_v[1]).T
    slope, slope_t, basis_t = parts_of(slope), parts_of(slope_t), parts_of(basis_t)
    lane = lax.broadcasted_iota(jnp.int32, (32, NC), 1)
    row = lax.broadcasted_iota(jnp.int32, (32, NC), 0)
    picked = jnp.where(lane == row + 32 * i, jnp.broadcast_to(cycle_ref[...], (32, NC)), 0.0)
    weight = 1.0 / (axial_ref[...] + jnp.sum(picked, axis=1, keepdims=True) + radial[j])

    hear(0)
    tell_z(1, 2)
    hear(2)
    tell_ax(3, 2)
    for copy in copies[6:]:
        copy.wait_recv()
    not_first, not_last = i > 0, i < NX - 1
    for ref, cols, left in ((cleft, slice(0, 128), True), (cright, slice(640, 768), False)):
        fields = unpack_columns([ref[t] for t in range(4)], left)
        for p in range(3):
            dext[p, 8:40, cols] = fields[p]
        for n in range(9):
            hext[n, 8:40, cols] = fields[3 + n]
        sext[8:40, cols] = fields[12]
    for copy in copies[:6]:
        copy.wait_recv()
    for side, (ref, d0, h0, there) in enumerate(((rtop, 6, 7, not_first), (rbot, 40, 40, not_last))):
        whole = jnp.concatenate([corner[side, 0], ref[...], corner[side, 1]], axis=1)
        whole = jnp.where(there, whole, 0.0)
        for p in range(3):
            dext[p, d0 : d0 + 2, :] = whole[2 * p : 2 * p + 2]
        for n in range(9):
            hext[n, h0 : h0 + 1, :] = whole[6 + n : 7 + n]
        sext[h0 : h0 + 1, :] = whole[15:16]

    windows = [(dext[p, 6:46, :], dext[p, 7:47, :], dext[p, 8:48, :]) for p in range(3)]
    grads = gradients(windows, slope_t)
    inside = lax.broadcasted_iota(jnp.int32, (40, 128), 0)
    keep = ((inside > 0) | not_first) & ((inside < 33) | not_last)
    factor = [1.0 + sext[7:47, 128 * t : 128 * (t + 1)] for t in range(6)]

    def couple(m):
        for t in range(6):
            cols = slice(128 * t, 128 * (t + 1))
            total = modulus[m, 0] * grads[0][:, cols]
            for n in range(1, 9):
                total = total + modulus[m, n] * grads[n][:, cols]
            stress_v[m, :, cols] = jnp.where(keep, factor[t] * total + hext[m, 7:47, cols], 0.0)

    def stress(m):
        return stress_v[m, 0:32, :], stress_v[m, 1:33, :], stress_v[m, 2:34, :]

    y_hi, x = lax.div(i, 4), lax.rem(i, 4)
    y_lo, z, core = lax.div(j, 16), lax.rem(lax.div(j, 2), 8), lax.rem(j, 2)
    at_y = [16 * lax.rem(y_lo + dy, 2) for dy in range(2)]
    at_z = [2 * lax.rem(z + dz, 8) for dz in range(8)]
    at_core = [lax.rem(core + dc, 2) for dc in range(2)]
    at_y_hi = [4 * lax.rem(y_hi + dy, 4) for dy in range(4)]
    at_x = [lax.rem(x + dx, 4) for dx in range(4)]
    far_circ = [at_y[dy] + at_z[dz] + at_core[dc] for dz in (4, 3, 5, 2, 6, 1, 7, 0) for dy in (1, 0) for dc in (1, 0)][:-1]
    far_ax = [at_y_hi[dy] + at_x[dx] for dy in (2, 1, 3, 0) for dx in (2, 1, 3, 0)][:-1]

    def start(k, p, src, dst, on_circ):
        me = j if on_circ else i
        for d in far_circ if on_circ else far_ax:
            pltpu.make_async_remote_copy(
                src_ref=src.at[p, d], dst_ref=dst.at[p, me], send_sem=a2a_send.at[k], recv_sem=a2a_recv.at[k, p],
                device_id=(i, d) if on_circ else (d, j), device_id_type=MESH,
            ).start()
        pltpu.make_async_copy(src.at[p, me], dst.at[p, me], a2a_recv.at[k, p]).start()

    def arrived(k, p, dst):
        pltpu.make_async_copy(dst.at[p], dst.at[p], a2a_recv.at[k, p]).wait()

    for p in range(3):
        for m in (p, 3 + p, 6 + p):
            couple(m)
        near, far = pulled(load_v[p], stress, p)
        mixed = dot3_t(*basis_t, near - dot3(far, *slope))
        for cl in range(4):
            s1[p, :, cl, :] = mixed[32 * cl : 32 * cl + 32]
        if p == 0:
            hear(1)
        start(0, p, s1, r1, True)

    hear(3)
    tell_ax(4, 4)
    table_copies[0].wait()
    for p in range(3):
        arrived(0, p, r1)
        line = jnp.concatenate([r1[p, :, cl, :] for cl in range(4)], axis=0)
        for it, four in enumerate(cycle_forward(line, table_v[0, 0], table_v[0, 1])):
            for i4 in range(4):
                s2[p, 4 * it + i4] = four[i4]
        if p == 0:
            hear(4)
        start(1, p, s2, r2, False)

    table_copies[1].wait()
    table_copies[2].wait()
    for p in range(3):
        arrived(1, p, r2)
        line = r2[p].reshape(128, 128)
        solved = axial_solve(line, weight, (table_v[1, 0], table_v[1, 1]), (table_v[2, 0], table_v[2, 1]))
        s3[p] = solved.reshape(NX, 8, 128)
        start(2, p, s3, r3, False)

    table_copies[3].wait()
    for p in range(3):
        arrived(2, p, r3)
        blocks = [[r3[p, 4 * it + i4] for i4 in range(4)] for it in range(4)]
        y = cycle_inverse(blocks, table_v[3, 0], table_v[3, 1])
        for c4 in range(4):
            s4[p, :, c4, :] = y[:, 128 * c4 : 128 * (c4 + 1)]
        start(3, p, s4, r4, True)

    for p in range(3):
        arrived(3, p, r4)
        line = jnp.concatenate([r4[p, :, c4, :] for c4 in range(4)], axis=0)
        out_v[128 * p : 128 * (p + 1), :] = dot3(line.T, *basis_t)

    for copy in copies:
        copy.wait_send()
    for k, (ref, count) in enumerate(((s1, NJ), (s2, NX), (s3, NX), (s4, NJ))):
        sent = ref.at[:, pl.ds(0, count - 1)]
        pltpu.make_async_copy(sent, sent, a2a_send.at[k]).wait()


def solution(mesh):
    table = tables()

    def body(displace, load, history, stiffen, modulus, slope, basis, axial, cycle, radial):
        hbm = pl.BlockSpec(memory_space=pltpu.HBM)
        dma = pltpu.SemaphoreType.DMA
        out = pl.pallas_call(
            kernel,
            out_shape=pltpu.VMEM((384, 128), F32),
            in_specs=[hbm] * 11,
            out_specs=pl.BlockSpec(memory_space=pltpu.VMEM),
            scratch_shapes=[
                pltpu.VMEM((R, R), F32),
                pltpu.VMEM((R, R), F32),
                pltpu.VMEM((1, NA), F32),
                pltpu.VMEM((1, NC), F32),
                pltpu.SMEM((9, 9), F32),
                pltpu.SMEM((R,), F32),
                pltpu.VMEM((3, 48, 768), F32),
                pltpu.VMEM((9, 48, 768), F32),
                pltpu.VMEM((48, 768), F32),
                pltpu.VMEM((3, 32, 512), F32),
                pltpu.VMEM((4, 2, 512, 512), BF16),
                pltpu.VMEM((2, 32, 128), F32),
                pltpu.VMEM((2, 16, 512), F32),
                pltpu.VMEM((2, 4, 32, 128), F32),
                pltpu.VMEM((16, 512), F32),
                pltpu.VMEM((16, 512), F32),
                pltpu.VMEM((4, 32, 128), F32),
                pltpu.VMEM((4, 32, 128), F32),
                pltpu.VMEM((2, 2, 16, 128), F32),
                pltpu.VMEM((9, 40, 768), F32),
                pltpu.VMEM((3, NJ, 4, 128), F32),
                pltpu.VMEM((3, NJ, 4, 128), F32),
                pltpu.VMEM((3, NX, 8, 128), F32),
                pltpu.VMEM((3, NX, 8, 128), F32),
                pltpu.VMEM((3, NX, 8, 128), F32),
                pltpu.VMEM((3, NX, 8, 128), F32),
                pltpu.VMEM((3, NJ, 4, 128), F32),
                pltpu.VMEM((3, NJ, 4, 128), F32),
                dma((10,)),
                dma((4,)),
                dma((8,)),
                dma((8,)),
                dma((4,)),
                dma((4, 3)),
                pltpu.SemaphoreType.REGULAR((5,)),
            ],
            compiler_params=pltpu.CompilerParams(
                collective_id=0, has_side_effects=True, vmem_limit_bytes=60 * 1024 * 1024
            ),
        )(
            displace, load, history, stiffen, jnp.asarray(table), slope, basis,
            axial.reshape(1, NA), cycle.reshape(1, NC), modulus, radial,
        )
        return out.reshape(3, 1, NC * R)

    return jax.shard_map(
        body,
        mesh=mesh,
        in_specs=(
            P(None, "ax", "circ"),
            P(None, "ax", "circ"),
            P(None, "ax", "circ"),
            P("ax", "circ"),
            P(),
            P(),
            P(),
            P(),
            P(),
            P(),
        ),
        out_specs=P(None, ("ax", "circ"), None),
        check_vma=False,
    )
```

```python
import math

import jax
import jax.numpy as jnp
import ml_dtypes
import numpy as np
from jax import lax
from jax.experimental import pallas as pl
from jax.experimental.pallas import tpu as pltpu
from jax.sharding import PartitionSpec as P

NA = 512
NC = 512
R = 32
NX = 16
NJ = 32
F32 = jnp.float32
BF16 = jnp.bfloat16
MESH = pl.DeviceIdType.MESH


def cycle_table():
    col = np.arange(NC)[:, None]
    mode = np.arange(NC)[None, :]
    half = NC // 2
    folded = np.where(mode <= half, mode, mode - half)
    shift = np.where(mode <= half, 0.0, 0.5 * np.pi)
    scale = np.where((mode == 0) | (mode == half), math.sqrt(1.0 / NC), math.sqrt(2.0 / NC))
    return np.cos((col * folded % NC) * (2.0 * np.pi / NC) - shift) * scale


def axial_table():
    first = (np.arange(NA) + 1)[:, None]
    mode = (np.arange(NA) + 1)[None, :]
    return np.sin((first * mode % (2 * (NA + 1))) * (np.pi / (NA + 1))) * math.sqrt(2.0 / (NA + 1))


def two_parts(table):
    table = table.astype(np.float32)
    high = table.astype(ml_dtypes.bfloat16)
    low = (table - high.astype(np.float32)).astype(ml_dtypes.bfloat16)
    return np.stack([high, low])


def tables():
    cyc, axi = cycle_table(), axial_table()
    q, cl, j = np.meshgrid(np.arange(4), np.arange(4), np.arange(NJ), indexing="ij")
    cycle_in = cyc[(16 * j + 4 * q + cl).reshape(-1)]
    a4, i, ah = np.meshgrid(np.arange(4), np.arange(NX), np.arange(8), indexing="ij")
    perm = (32 * i + 8 * a4 + ah).reshape(-1)
    c4, cg = np.meshgrid(np.arange(4), np.arange(128), indexing="ij")
    cycle_out = cyc.T[:, (4 * cg + c4).reshape(-1)]
    return np.stack([two_parts(cycle_in), two_parts(axi[perm]), two_parts(axi[:, perm]), two_parts(cycle_out)])


def roll(x, shift):
    return pltpu.roll(x, shift % x.shape[-1], x.ndim - 1)


def parts_of(x):
    high = x.astype(BF16)
    return high, (x - high.astype(F32)).astype(BF16)


def mm(a, b):
    return jnp.dot(a, b, preferred_element_type=F32)


def mm_t(a, b):
    return lax.dot_general(a, b, (((1,), (1,)), ((), ())), preferred_element_type=F32)


def dot3(x, high, low):
    xh, xl = parts_of(x)
    n = x.shape[0]
    both = mm(jnp.concatenate([xh, xl], axis=0), high)
    return both[:n] + (both[n:] + mm(xh, low))


def dot3_t(high, low, x):
    xh, xl = parts_of(x)
    n = high.shape[0]
    both = mm_t(jnp.concatenate([high, low], axis=0), xh)
    return both[:n] + (both[n:] + mm_t(high, xl))


def block_diag(x):
    wide = x + roll(x, 32)
    wide = wide + roll(wide, 64)
    full = jnp.concatenate([wide] * 4, axis=0)
    row = lax.broadcasted_iota(jnp.int32, (128, 128), 0) // 32
    lane = lax.broadcasted_iota(jnp.int32, (128, 128), 1) // 32
    return jnp.where(row == lane, full, 0.0)


def swap_groups(v):
    group = lax.broadcasted_iota(jnp.int32, v[0].shape, 1) // 32
    low_half = group < 2
    a0 = jnp.where(low_half, v[0], roll(v[2], 64))
    a2 = jnp.where(low_half, roll(v[0], 64), v[2])
    a1 = jnp.where(low_half, v[1], roll(v[3], 64))
    a3 = jnp.where(low_half, roll(v[1], 64), v[3])
    even = (group % 2) == 0
    u0 = jnp.where(even, a0, roll(a1, 32))
    u1 = jnp.where(even, roll(a0, -32), a1)
    u2 = jnp.where(even, a2, roll(a3, 32))
    u3 = jnp.where(even, roll(a2, -32), a3)
    return [u0, u1, u2, u3]


def tiles(x):
    return [x[:, 128 * t : 128 * (t + 1)] for t in range(x.shape[1] // 128)]


def rows(x, n):
    return [x[n * t : n * (t + 1)] for t in range(x.shape[0] // n)]


def smooth_a(up, mid, down):
    return (up + 4.0 * mid + down) * (1.0 / 6.0)


def slope_a(up, down):
    return (down - up) * 0.5


def smooth_c(x):
    return (roll(x, 32) + 4.0 * x + roll(x, -32)) * (1.0 / 6.0)


def slope_c(x):
    return (roll(x, -32) - roll(x, 32)) * 0.5


def gradients(windows, slope_t):
    first, second, plain = [], [], []
    for up, mid, down in windows:
        first.append(smooth_c(slope_a(up, down)))
        smooth = smooth_a(up, mid, down)
        second.append(slope_c(smooth))
        plain.append(smooth_c(smooth))
    stacked = jnp.concatenate([t for x in plain for t in tiles(x)], axis=0)
    mixed = rows(dot3(stacked, *slope_t), 40)
    third = [jnp.concatenate(mixed[6 * p : 6 * p + 6], axis=1) for p in range(3)]
    return first + second + third


def pulled(load, stress, p):
    up, _, down = stress(p)
    part = smooth_c(slope_a(up, down))
    part = part + slope_c(smooth_a(*stress(3 + p)))
    third = smooth_c(smooth_a(*stress(6 + p)))
    near = load + part[:, 128:640]
    return jnp.concatenate(tiles(near), axis=0), jnp.concatenate(tiles(third[:, 128:640]), axis=0)


def cycle_forward(x, high, low):
    y = dot3(jnp.concatenate(rows(x.T, 32), axis=1), high, low)
    return [swap_groups(rows(t, 8)) for t in tiles(y)]


def axial_solve(x, weight, forward, inverse):
    modes = dot3(jnp.concatenate(rows(x.T, 32), axis=1), *forward)
    y = dot3(modes * weight, *inverse)
    return jnp.concatenate(tiles(y), axis=0).T


def cycle_inverse(blocks, high, low):
    cols = [jnp.concatenate(swap_groups(four), axis=0) for four in blocks]
    return dot3(jnp.concatenate(cols, axis=1), high, low)


def pack_columns(fields, last):
    lane = lax.broadcasted_iota(jnp.int32, (32, 128), 1)

    def move(x, width, at):
        start = 128 - width if last else 0
        return roll(x, at - start) if at != start else x

    two = jnp.where(lane < 64, move(fields[0], 64, 0), move(fields[1], 64, 64))
    mixed = jnp.where(lane < 96, move(fields[3], 32, 64), move(fields[4], 32, 96))
    out = [two, jnp.where(lane < 64, move(fields[2], 64, 0), mixed)]
    for first in (5, 9):
        low = jnp.where(lane < 32, move(fields[first], 32, 0), move(fields[first + 1], 32, 32))
        high = jnp.where(lane < 96, move(fields[first + 2], 32, 64), move(fields[first + 3], 32, 96))
        out.append(jnp.where(lane < 64, low, high))
    return out


def unpack_columns(packed, last):
    def move(x, width, at):
        end = 128 - width if last else 0
        return roll(x, end - at) if at != end else x

    out = [move(packed[0], 64, 0), move(packed[0], 64, 64), move(packed[1], 64, 0)]
    out += [move(packed[1], 32, 64), move(packed[1], 32, 96)]
    for t in (2, 3):
        out += [move(packed[t], 32, 32 * g) for g in range(4)]
    return out


def kernel(
    displace, load, history, stiffen, table, slope_hbm, basis_hbm, axial_hbm, cycle_hbm, modulus_hbm, radial_hbm,
    out_v,
    slope_ref, basis_ref, axial_ref, cycle_ref, modulus, radial,
    dext, hext, sext, load_v, table_v, pad_v, rsend, csend, rtop, rbot, cleft, cright, corner, stress_v,
    s1, r1, s2, r2, s3, r3, s4, r4,
    in_sem, table_sem, halo_send, halo_recv, a2a_send, a2a_recv, known,
):
    i = lax.axis_index("ax")
    j = lax.axis_index("circ")
    up_i, down_i = lax.rem(i + NX - 1, NX), lax.rem(i + 1, NX)
    left_j, right_j = lax.rem(j + NJ - 1, NJ), lax.rem(j + 1, NJ)

    own = [
        pltpu.make_async_copy(displace, dext.at[:, 8:40, 128:640], in_sem.at[0]),
        pltpu.make_async_copy(history, hext.at[:, 8:40, 128:640], in_sem.at[1]),
        pltpu.make_async_copy(stiffen, sext.at[8:40, 128:640], in_sem.at[2]),
        pltpu.make_async_copy(slope_hbm, slope_ref, in_sem.at[3]),
        pltpu.make_async_copy(basis_hbm, basis_ref, in_sem.at[4]),
        pltpu.make_async_copy(axial_hbm, axial_ref, in_sem.at[5]),
        pltpu.make_async_copy(cycle_hbm, cycle_ref, in_sem.at[6]),
        pltpu.make_async_copy(modulus_hbm, modulus, in_sem.at[7]),
        pltpu.make_async_copy(radial_hbm, radial, in_sem.at[8]),
        pltpu.make_async_copy(load, load_v, in_sem.at[9]),
    ]
    for copy in own:
        copy.start()
    table_copies = [pltpu.make_async_copy(table.at[k], table_v.at[k], table_sem.at[k]) for k in range(4)]

    barrier = pltpu.get_barrier_semaphore()

    def near_z(side, step):
        y_lo, z, core = lax.div(j, 16), lax.rem(lax.div(j, 2), 8), lax.rem(j, 2)
        y_lo = lax.rem(y_lo + side // 2, 2)
        core = lax.rem(core + side % 2, 2)
        return y_lo * 16 + lax.rem(z + step, 8) * 2 + core

    def signal(sem, di, dj):
        pl.semaphore_signal(sem, inc=1, device_id=(di, dj), device_id_type=MESH)

    for di in (up_i, down_i):
        for dj in (left_j, right_j, j):
            signal(barrier, di, dj)
    for side in range(4):
        for step in (7, 1, 0):
            if side or step:
                signal(barrier, i, near_z(side, step))

    for copy in own[:3]:
        copy.wait()
    for side, (d0, h0) in enumerate(((8, 8), (38, 39))):
        for p in range(3):
            rsend[side, 2 * p : 2 * p + 2, :] = dext[p, d0 : d0 + 2, 128:640]
        for n in range(9):
            rsend[side, 6 + n : 7 + n, :] = hext[n, h0 : h0 + 1, 128:640]
        rsend[side, 15:16, :] = sext[h0 : h0 + 1, 128:640]

    for side, cols in enumerate((slice(128, 256), slice(512, 640))):
        edge = [dext[p, 8:40, cols] for p in range(3)] + [hext[n, 8:40, cols] for n in range(9)] + [sext[8:40, cols]]
        for t, value in enumerate(pack_columns(edge, side == 1)):
            csend[side, t] = value

    pl.semaphore_wait(barrier, 17)

    copies = []

    def send(src, dst, device):
        k = len(copies)
        copy = pltpu.make_async_remote_copy(
            src_ref=src, dst_ref=dst, send_sem=halo_send.at[k], recv_sem=halo_recv.at[k],
            device_id=device, device_id_type=MESH,
        )
        copy.start()
        copies.append(copy)

    send(rsend.at[1, :, 384:512], corner.at[0, 0], (down_i, right_j))
    send(rsend.at[1, :, 0:128], corner.at[0, 1], (down_i, left_j))
    send(rsend.at[0, :, 384:512], corner.at[1, 0], (up_i, right_j))
    send(rsend.at[0, :, 0:128], corner.at[1, 1], (up_i, left_j))
    send(rsend.at[1], rtop, (down_i, j))
    send(rsend.at[0], rbot, (up_i, j))
    send(csend.at[1], cleft, (i, right_j))
    send(csend.at[0], cright, (i, left_j))
    for copy in table_copies:
        copy.start()

    def tell_z(k, step):
        for way in (step, 8 - step):
            signal(known.at[k], i, near_z(0, way))

    def tell_ax(k, step):
        for way in (step, NX - step):
            signal(known.at[k], lax.rem(i + way, NX), j)

    def hear(k):
        pl.semaphore_wait(known.at[k], 2)

    tell_z(0, 1)
    tell_ax(2, 1)
    for copy in own[3:]:
        copy.wait()
    pad_v[...] = jnp.zeros_like(pad_v)
    pad_v[0, :, 0:32] = slope_ref[...]
    pad_v[1, :, 0:32] = basis_ref[...]
    slope = block_diag(pad_v[0])
    slope_t = slope.T
    basis_t = block_diag(pad_v[1]).T
    slope, slope_t, basis_t = parts_of(slope), parts_of(slope_t), parts_of(basis_t)
    lane = lax.broadcasted_iota(jnp.int32, (32, NC), 1)
    row = lax.broadcasted_iota(jnp.int32, (32, NC), 0)
    picked = jnp.where(lane == row + 32 * i, jnp.broadcast_to(cycle_ref[...], (32, NC)), 0.0)
    weight = 1.0 / (axial_ref[...] + jnp.sum(picked, axis=1, keepdims=True) + radial[j])

    hear(0)
    tell_z(1, 2)
    hear(2)
    tell_ax(3, 2)
    for copy in copies[6:]:
        copy.wait_recv()
    not_first, not_last = i > 0, i < NX - 1
    for ref, cols, left in ((cleft, slice(0, 128), True), (cright, slice(640, 768), False)):
        fields = unpack_columns([ref[t] for t in range(4)], left)
        for p in range(3):
            dext[p, 8:40, cols] = fields[p]
        for n in range(9):
            hext[n, 8:40, cols] = fields[3 + n]
        sext[8:40, cols] = fields[12]
    for copy in copies[:6]:
        copy.wait_recv()
    for side, (ref, d0, h0, there) in enumerate(((rtop, 6, 7, not_first), (rbot, 40, 40, not_last))):
        whole = jnp.concatenate([corner[side, 0], ref[...], corner[side, 1]], axis=1)
        whole = jnp.where(there, whole, 0.0)
        for p in range(3):
            dext[p, d0 : d0 + 2, :] = whole[2 * p : 2 * p + 2]
        for n in range(9):
            hext[n, h0 : h0 + 1, :] = whole[6 + n : 7 + n]
        sext[h0 : h0 + 1, :] = whole[15:16]

    windows = [(dext[p, 6:46, :], dext[p, 7:47, :], dext[p, 8:48, :]) for p in range(3)]
    grads = gradients(windows, slope_t)
    inside = lax.broadcasted_iota(jnp.int32, (40, 128), 0)
    keep = ((inside > 0) | not_first) & ((inside < 33) | not_last)
    factor = [1.0 + sext[7:47, 128 * t : 128 * (t + 1)] for t in range(6)]

    def couple(m):
        for t in range(6):
            cols = slice(128 * t, 128 * (t + 1))
            total = modulus[m, 0] * grads[0][:, cols]
            for n in range(1, 9):
                total = total + modulus[m, n] * grads[n][:, cols]
            stress_v[m, :, cols] = jnp.where(keep, factor[t] * total + hext[m, 7:47, cols], 0.0)

    def stress(m):
        return stress_v[m, 0:32, :], stress_v[m, 1:33, :], stress_v[m, 2:34, :]

    y_hi, x = lax.div(i, 4), lax.rem(i, 4)
    y_lo, z, core = lax.div(j, 16), lax.rem(lax.div(j, 2), 8), lax.rem(j, 2)
    at_y = [16 * lax.rem(y_lo + dy, 2) for dy in range(2)]
    at_z = [2 * lax.rem(z + dz, 8) for dz in range(8)]
    at_core = [lax.rem(core + dc, 2) for dc in range(2)]
    at_y_hi = [4 * lax.rem(y_hi + dy, 4) for dy in range(4)]
    at_x = [lax.rem(x + dx, 4) for dx in range(4)]
    far_circ = [at_y[dy] + at_z[dz] + at_core[dc] for dz in (4, 3, 5, 2, 6, 1, 7, 0) for dy in (1, 0) for dc in (1, 0)][:-1]
    far_ax = [at_y_hi[dy] + at_x[dx] for dy in (2, 1, 3, 0) for dx in (2, 1, 3, 0)][:-1]

    def start(k, p, src, dst, on_circ):
        me = j if on_circ else i
        for d in far_circ if on_circ else far_ax:
            pltpu.make_async_remote_copy(
                src_ref=src.at[p, d], dst_ref=dst.at[p, me], send_sem=a2a_send.at[k], recv_sem=a2a_recv.at[k, p],
                device_id=(i, d) if on_circ else (d, j), device_id_type=MESH,
            ).start()
        pltpu.make_async_copy(src.at[p, me], dst.at[p, me], a2a_recv.at[k, p]).start()

    def arrived(k, p, dst):
        pltpu.make_async_copy(dst.at[p], dst.at[p], a2a_recv.at[k, p]).wait()

    for p in range(3):
        for m in (p, 3 + p, 6 + p):
            couple(m)
        near, far = pulled(load_v[p], stress, p)
        mixed = dot3_t(*basis_t, near - dot3(far, *slope))
        for cl in range(4):
            s1[p, :, cl, :] = mixed[32 * cl : 32 * cl + 32]
        if p == 0:
            hear(1)
        start(0, p, s1, r1, True)

    hear(3)
    tell_ax(4, 4)
    table_copies[0].wait()
    for p in range(3):
        arrived(0, p, r1)
        line = jnp.concatenate([r1[p, :, cl, :] for cl in range(4)], axis=0)
        for it, four in enumerate(cycle_forward(line, table_v[0, 0], table_v[0, 1])):
            for i4 in range(4):
                s2[p, 4 * it + i4] = four[i4]
        if p == 0:
            hear(4)
        start(1, p, s2, r2, False)

    table_copies[1].wait()
    table_copies[2].wait()
    for p in range(3):
        arrived(1, p, r2)
        line = r2[p].reshape(128, 128)
        solved = axial_solve(line, weight, (table_v[1, 0], table_v[1, 1]), (table_v[2, 0], table_v[2, 1]))
        s3[p] = solved.reshape(NX, 8, 128)
        start(2, p, s3, r3, False)

    table_copies[3].wait()
    for p in range(3):
        arrived(2, p, r3)
        blocks = [[r3[p, 4 * it + i4] for i4 in range(4)] for it in range(4)]
        y = cycle_inverse(blocks, table_v[3, 0], table_v[3, 1])
        for c4 in range(4):
            s4[p, :, c4, :] = y[:, 128 * c4 : 128 * (c4 + 1)]
        start(3, p, s4, r4, True)

    for p in range(3):
        arrived(3, p, r4)
        line = jnp.concatenate([r4[p, :, c4, :] for c4 in range(4)], axis=0)
        out_v[128 * p : 128 * (p + 1), :] = dot3(line.T, *basis_t)

    for copy in copies:
        copy.wait_send()
    for k, (ref, count) in enumerate(((s1, NJ), (s2, NX), (s3, NX), (s4, NJ))):
        sent = ref.at[:, pl.ds(0, count - 1)]
        pltpu.make_async_copy(sent, sent, a2a_send.at[k]).wait()


def solution(mesh):
    table = tables()

    def body(displace, load, history, stiffen, modulus, slope, basis, axial, cycle, radial):
        hbm = pl.BlockSpec(memory_space=pltpu.HBM)
        dma = pltpu.SemaphoreType.DMA
        out = pl.pallas_call(
            kernel,
            out_shape=pltpu.VMEM((384, 128), F32),
            in_specs=[hbm] * 11,
            out_specs=pl.BlockSpec(memory_space=pltpu.VMEM),
            scratch_shapes=[
                pltpu.VMEM((R, R), F32),
                pltpu.VMEM((R, R), F32),
                pltpu.VMEM((1, NA), F32),
                pltpu.VMEM((1, NC), F32),
                pltpu.SMEM((9, 9), F32),
                pltpu.SMEM((R,), F32),
                pltpu.VMEM((3, 48, 768), F32),
                pltpu.VMEM((9, 48, 768), F32),
                pltpu.VMEM((48, 768), F32),
                pltpu.VMEM((3, 32, 512), F32),
                pltpu.VMEM((4, 2, 512, 512), BF16),
                pltpu.VMEM((2, 32, 128), F32),
                pltpu.VMEM((2, 16, 512), F32),
                pltpu.VMEM((2, 4, 32, 128), F32),
                pltpu.VMEM((16, 512), F32),
                pltpu.VMEM((16, 512), F32),
                pltpu.VMEM((4, 32, 128), F32),
                pltpu.VMEM((4, 32, 128), F32),
                pltpu.VMEM((2, 2, 16, 128), F32),
                pltpu.VMEM((9, 40, 768), F32),
                pltpu.VMEM((3, NJ, 4, 128), F32),
                pltpu.VMEM((3, NJ, 4, 128), F32),
                pltpu.VMEM((3, NX, 8, 128), F32),
                pltpu.VMEM((3, NX, 8, 128), F32),
                pltpu.VMEM((3, NX, 8, 128), F32),
                pltpu.VMEM((3, NX, 8, 128), F32),
                pltpu.VMEM((3, NJ, 4, 128), F32),
                pltpu.VMEM((3, NJ, 4, 128), F32),
                dma((10,)),
                dma((4,)),
                dma((8,)),
                dma((8,)),
                dma((4,)),
                dma((4, 3)),
                pltpu.SemaphoreType.REGULAR((5,)),
            ],
            compiler_params=pltpu.CompilerParams(
                collective_id=0, has_side_effects=True, vmem_limit_bytes=60 * 1024 * 1024
            ),
        )(
            displace, load, history, stiffen, jnp.asarray(table), slope, basis,
            axial.reshape(1, NA), cycle.reshape(1, NC), modulus, radial,
        )
        return out.reshape(3, 1, NC * R)

    return jax.shard_map(
        body,
        mesh=mesh,
        in_specs=(
            P(None, "ax", "circ"),
            P(None, "ax", "circ"),
            P(None, "ax", "circ"),
            P("ax", "circ"),
            P(),
            P(),
            P(),
            P(),
            P(),
            P(),
        ),
        out_specs=P(None, ("ax", "circ"), None),
        check_vma=False,
    )
```
